512 devices in a mesh: orb: 32 (over z, core), vec: 16 (over y, x).
Axes of the slice: x: 4, y: 4, z: 16, core: 2. Of those that a mesh axis runs over, the one named last changes fastest.
Arguments:
- orbitals: bfloat16 [32, 96, 9216], P('orb'), may hold values from -6 to 6
- energies: float32 [32], P('orb'), may hold values from -1 to 0
- trial_potential: bfloat16 [16, 96, 9216], P('vec', 'orb'), may hold values from -6 to 6
- local_potential: bfloat16 [96, 9216], P('orb'), may hold values from 0.5 to 2
Outputs:
- ortho: float32 [16, 96, 9216], P('vec', 'orb')
- factor: float32 [16, 16], replicated
The draws below stay inside these ranges and needn't reach their ends.
All inputs are finite; a program needn't handle non-finite values.
Results may differ from the reference program's by a relative error of at most 0.0003.
Values may be sent and summed in bfloat16 or wider, within the bound.
A program may use at most 64 MiB of HBM per device.

```python
import jax
import jax.numpy as jnp
from jax import lax

NZ = 96
NY = 96
NX = 96
NYX = 9216
STEPS = 4
NORB = 32
NV = 16


def level_of(own_key, dims, cuts, least, largest):
    loudness = 1.0
    for position, shards_of in cuts:
        steps = jax.random.uniform(jax.random.fold_in(jax.random.fold_in(own_key, 6), position), (shards_of,), jnp.float32, least / len(cuts), largest / len(cuts))
        loudness = loudness * jnp.repeat(jnp.exp(steps), dims[position] // shards_of).reshape((-1,) + (1,) * (len(dims) - 1 - position))
    return loudness


def normal_values(rng, shape, width, bound, split=(), kind=jnp.bfloat16):
    drawn = jax.random.normal(rng, shape, jnp.float32) * width
    if len(split) > 0:
        drawn = level_of(rng, shape, split, -0.22, 0.18) * drawn
    return jnp.clip(drawn, min=-bound, max=bound).astype(kind)


def setup_inputs(seed: int = 0) -> dict:
    seeds = jax.random.split(jax.random.key(seed), 5)
    orbitals = normal_values(seeds[0], (NORB, NZ, NYX), 1.0, 6.0, ((0, 32),))
    energies = jnp.clip(-1.0 + 1.0 * jax.random.uniform(seeds[1], (NORB,), jnp.float32) ** level_of(seeds[1], (NORB,), ((0, 32),), -0.2, 0.2), -1.0, 0.0)
    trial_potential = normal_values(seeds[2], (NV, NZ, NYX), 1.0, 6.0, ((0, 16), (1, 32)))
    local_potential = jnp.clip(0.5 + 1.5 * jax.random.uniform(seeds[3], (NZ, NYX), jnp.float32) ** level_of(seeds[3], (NZ, NYX), ((0, 32),), -0.2, 0.2), 0.5, 2.0).astype(jnp.bfloat16)
    return {"orbitals": orbitals, "energies": energies, "trial_potential": trial_potential, "local_potential": local_potential}


def neighbours(field):
    depth, flat = field.shape
    zero_plane = jnp.zeros((1, flat), field.dtype)
    total = jnp.concatenate([zero_plane, field[:-1]], 0) + jnp.concatenate([field[1:], zero_plane], 0)
    zero_rows = jnp.zeros((depth, NX), field.dtype)
    total = total + jnp.concatenate([zero_rows, field[:, :-NX]], 1) + jnp.concatenate([field[:, NX:], zero_rows], 1)
    column = jnp.arange(flat) % NX
    zero_col = jnp.zeros((depth, 1), field.dtype)
    left = jnp.concatenate([zero_col, field[:, :-1]], 1) * (column > 0).astype(field.dtype)
    right = jnp.concatenate([field[:, 1:], zero_col], 1) * (column < NX - 1).astype(field.dtype)
    return total + left + right

def solve(psi, perturb, potential, energy):
    diag = 3.25 + potential - energy
    source = -perturb * psi
    answer = jnp.zeros_like(psi)
    for step in range(STEPS):
        weight = 1.0 / (1.0 + 0.8 * jnp.cos(jnp.pi * (2 * step + 1) / (2 * STEPS)))
        applied = diag * answer - 0.5 * neighbours(answer)
        answer = answer + weight * (source - applied) / diag
    return answer

def sine_basis(count):
    index = jnp.arange(count, dtype=jnp.float32) + 1.0
    return jnp.sqrt(2.0 / (count + 1)) * jnp.sin(jnp.pi * index[:, None] * index[None, :] / (count + 1))

def eigen_values(count):
    index = jnp.arange(count, dtype=jnp.float32) + 1.0
    return 2.0 - 2.0 * jnp.cos(jnp.pi * index / (count + 1))

def transform(cube):
    high = lax.Precision.HIGHEST
    cube = jnp.einsum('zyx,cx->zyc', cube, sine_basis(NX), precision=high)
    cube = jnp.einsum('zyc,by->zbc', cube, sine_basis(NY), precision=high)
    return jnp.einsum('zbc,az->abc', cube, sine_basis(NZ), precision=high)

def coulomb(field):
    cube = transform(field.reshape(NZ, NY, NX))
    denom = eigen_values(NZ)[:, None, None] + eigen_values(NY)[None, :, None] + eigen_values(NX)[None, None, :]
    cube = cube * (jnp.sqrt(4.0 * jnp.pi) / jnp.sqrt(denom))
    return transform(cube).reshape(NZ, NYX)

def reference(orbitals, energies, trial_potential, local_potential):
    potential = local_potential.astype(jnp.float32)

    def one_vector(vector):
        perturb = vector.astype(jnp.float32)

        def add_orbital(index, total):
            psi = lax.dynamic_index_in_dim(orbitals, index, 0, keepdims=False).astype(jnp.float32)
            return total + psi * solve(psi, perturb, potential, energies[index])
        chi = lax.fori_loop(0, NORB, add_orbital, jnp.zeros((NZ, NYX), jnp.float32))
        return coulomb(chi * (4.0 / NORB))
    responses = lax.map(one_vector, trial_potential)
    flat = responses.reshape(NV, NZ * NYX)
    gram = jnp.dot(flat, flat.T, precision=lax.Precision.HIGHEST) / (NZ * NYX)
    lower = jnp.linalg.cholesky(gram)
    inverse = lax.linalg.triangular_solve(lower, jnp.eye(NV, dtype=jnp.float32), left_side=True, lower=True)
    ortho = jnp.dot(inverse, flat, precision=lax.Precision.HIGHEST)
    return (ortho.reshape(NV, NZ, NYX), lower.T)
```

```python
import jax
import jax.numpy as jnp
import numpy as np
from jax import lax
from jax.experimental import pallas as pl
from jax.experimental.pallas import tpu as pltpu
from jax.sharding import PartitionSpec as P

NZ = 96
NY = 96
NX = 96
NYX = 9216
NORB = 32
NV = 16
F32 = jnp.float32
BF16 = jnp.bfloat16
HIGH = lax.Precision.HIGHEST
T4 = 8.0 / 0.8**4 - 8.0 / 0.8**2 + 1.0
Q0 = (T4 - 1.0) / T4
Q2 = (8.0 / 0.8**4) / T4
SCALE = 4.0 / NORB
ZORDER = (0, 2, 1, 3)


def sine(n):
    i = np.arange(n, dtype=np.float64) + 1.0
    return np.sqrt(2.0 / (n + 1)) * np.sin(np.pi * i[:, None] * i[None, :] / (n + 1))


def tables():
    s = sine(96)
    row_y = np.arange(96)
    y_of = 4 * (row_y % 24) + row_y // 24
    sx = np.zeros((128, 128))
    for g in range(32):
        for r in range(3):
            sx[:96, 4 * g + r] = s[:, 3 * g + r]
    sy = np.zeros((128, 128))
    for w in range(16):
        for i in range(6):
            sy[8 * w + i, :96] = s[6 * w + i, y_of]
    kz = np.kron(s, np.eye(4))
    pick = np.zeros((128, 128))
    same = np.zeros((128, 128))
    for a in range(128):
        pick[a, a // 8] = 1.0
        for b in range(128):
            same[a, b] = float(a % 8 == b % 8)
    small = np.stack([sx, sx.T, sy, sy.T, pick, pick.T, same])
    return small.astype(np.float32), kz.astype(np.float32)


def offset(x, q):
    base = 8 * (q % 2)
    if q < 2:
        return base + x
    return (base + 16 - x + jnp.where(x == 0, 4, 0)) % 16


def unpack(packed, lane):
    f0, f1, f2 = packed[:, :128], packed[:, 128:256], packed[:, 256:]
    y0 = jnp.where(lane < 96, f0, 0.0)
    y1 = jnp.where(lane < 32, pltpu.roll(f0, 32, 1), jnp.where(lane < 96, pltpu.roll(f1, 32, 1), 0.0))
    y2 = jnp.where(lane < 64, pltpu.roll(f1, 64, 1), jnp.where(lane < 96, pltpu.roll(f2, 64, 1), 0.0))
    y3 = jnp.where(lane < 96, pltpu.roll(f2, 96, 1), 0.0)
    return y0, y1, y2, y3


def pack(y, lane):
    r1, r2, r3 = pltpu.roll(y[1], 96, 1), pltpu.roll(y[2], 64, 1), pltpu.roll(y[3], 32, 1)
    return (
        jnp.where(lane < 96, y[0], r1),
        jnp.where(lane < 64, r1, r2),
        jnp.where(lane < 32, r2, r3),
    )


def kernel(
    psi_in, pert, pot, energy, small, kz_hbm, damp, out, factor,
    kz, psi_all, en_all, pv, vf, potf, cf, pdf, psif, gf, hf, mf, acc,
    pk, rc, rd, rx, x1, y1, u1, w1, u2, w2, x2, y2, t1, t2,
    zs, zr, es, er, xs, xr, hs, hr, ys, yr, cs, rs, rr,
    a1s, a1r, b1s, b1r, b2s, b2r, g1s, g1r, g2s, g2r, a2s, a2r, ks,
):
    o = lax.axis_index("orb")
    v = lax.axis_index("vec")
    z, c = o // 2, o % 2
    y, x = v // 4, v % 4
    mate = 2 * z + 1 - c

    def copy(src, dst, send, recv, orb, vec):
        return pltpu.make_async_remote_copy(
            src_ref=src, dst_ref=dst, send_sem=send, recv_sem=recv,
            device_id={"orb": orb, "vec": vec}, device_id_type=pl.DeviceIdType.MESH,
        )

    barrier = pltpu.get_barrier_semaphore()

    def greet(orb, vec):
        pl.semaphore_signal(
            barrier, inc=1, device_id={"orb": orb, "vec": vec}, device_id_type=pl.DeviceIdType.MESH
        )

    @pl.loop(1, 32)
    def _(d):
        greet((o + d) % 32, v)

    @pl.loop(1, 16)
    def _(d):
        greet(o, (v + d) % 16)
        greet(mate, (v + d) % 16)

    load_kz = pltpu.make_async_copy(kz_hbm, kz, ks)
    load_kz.start()
    own = 1 + c
    pv[own, x] = pert[...]
    pv[own, 4] = pot[...]
    for f in (gf, hf, mf):
        f[:, :, :8, :] = jnp.zeros((12, 4, 8, 128), F32)
        f[:, :, 32:, :] = jnp.zeros((12, 4, 8, 128), F32)
    acc[...] = jnp.zeros(acc.shape, F32)
    pl.semaphore_wait(barrier, 61)

    def z_copy(q):
        return copy(psi_in.at[q], psi_all.at[y, q], zs.at[q], zr.at[q], 2 * ((z + 16 - offset(x, q)) % 16) + c, v)

    def e_copy(q):
        return copy(energy, en_all.at[q], es.at[q], er.at[q], 2 * ((z + 16 - offset(x, q)) % 16) + c, v)

    def x_copy(d):
        return copy(pert, pv.at[own, x], xs.at[d - 1], xr.at[d - 1], o, 4 * y + (x + d) % 4)

    for d in (2, 1, 3):
        x_copy(d).start()

    @pl.when(x != 0)
    def _():
        z_copy(0).start()
        e_copy(0).start()

    @pl.when(x == 0)
    def _():
        psi_all[y, 0] = psi_in[0]
        en_all[0] = energy[...]

    for q in ZORDER[1:]:
        z_copy(q).start()
        e_copy(q).start()

    far = 3 - 3 * c
    h_mate = copy(pv.at[own], pv.at[own], hs.at[0], hr.at[0], mate, v)
    h_next = copy(pv.at[own], pv.at[far], hs.at[1], hr.at[1], 2 * ((z + 2 * c + 15) % 16) + c, v)
    h_pass = copy(pv.at[far], pv.at[far], hs.at[2], hr.at[2], mate, v)
    for d in (1, 2, 3):
        x_copy(d).wait()
    h_next.start()
    h_mate.start()

    def y_copy(q, d):
        return copy(psi_all.at[y, q], psi_all.at[y, q], ys.at[3 * q + d - 1], yr.at[3 * q + d - 1], o, 4 * ((y + d) % 4) + x)

    def spread(q):
        def arrived():
            z_copy(q).wait()
            e_copy(q).wait()

        if q == 0:
            pl.when(x != 0)(arrived)
        else:
            arrived()
        for d in (2, 1, 3):
            y_copy(q, d).start()

    lane = lax.broadcasted_iota(jnp.int32, (24, 128), 1)

    def solve(q):
        for d in (1, 2, 3):
            y_copy(q, d).wait()
        level = en_all[q, 0:1, :]

        @pl.loop(0, 12)
        def _(p):
            plane = 6 * z - 3 + p
            half = jnp.where((plane >= 0) & (plane < NZ), 0.5, 0.0)
            psi = unpack(psi_all[p // 3, q, p % 3].astype(F32), lane)
            for s in range(4):
                inverse = 1.0 / (3.25 + potf[p, s] - level)
                cf[p, s] = jnp.where(lane < 96, half * inverse, 0.0)
                pdf[p, s] = -psi[s] * inverse
                psif[p, s] = psi[s]

        def stencil(f, p):
            mid = [f[p, s, 8:32, :] for s in range(4)]
            total = []
            for s in range(4):
                up = mid[s - 1] if s > 0 else f[p, 3, 7:31, :]
                down = mid[s + 1] if s < 3 else f[p, 0, 9:33, :]
                n = (f[p - 1, s, 8:32, :] + f[p + 1, s, 8:32, :]) + (up + down)
                n = n + (pltpu.roll(mid[s], 1, 1) + pltpu.roll(mid[s], 127, 1))
                total.append(cf[p, s] * n)
            return mid, total

        @pl.loop(0, 4)
        def _(k):
            @pl.loop(0, 12)
            def _(p):
                for s in range(4):
                    gf[p, s, 8:32, :] = vf[k, p, s] * pdf[p, s]

            @pl.loop(1, 11)
            def _(p):
                mid, total = stencil(gf, p)
                for s in range(4):
                    hf[p, s, 8:32, :] = mid[s] + total[s]

            @pl.loop(2, 10)
            def _(p):
                _, total = stencil(hf, p)
                for s in range(4):
                    mf[p, s, 8:32, :] = total[s]

            @pl.loop(3, 9)
            def _(p):
                _, total = stencil(mf, p)
                for s in range(4):
                    answer = (SCALE * Q0) * hf[p, s, 8:32, :] + (SCALE * Q2) * total[s]
                    acc[k, p - 3, s] = acc[k, p - 3, s] + psif[p, s] * answer

    spread(0)
    spread(2)
    h_next.wait()
    h_pass.start()
    h_mate.wait()
    spread(1)
    h_pass.wait()

    @pl.loop(0, 12)
    def _(p):
        slab, t = p // 3, p % 3
        for k in range(4):
            field = unpack(pv[slab, k, t].astype(F32), lane)
            for s in range(4):
                vf[k, p, s] = field[s]
        field = unpack(pv[slab, 4, t].astype(F32), lane)
        for s in range(4):
            potf[p, s] = field[s]

    solve(0)
    spread(3)
    solve(2)
    solve(1)
    solve(3)

    @pl.loop(0, 4)
    def _(k):
        for p in range(6):
            f = pack([acc[k, p, s] for s in range(4)], lane)
            for t in range(3):
                pk[p // 3, k, p % 3, :, 128 * t : 128 * t + 128] = f[t]

    half_copy = copy(pk.at[1 - c], rc, cs.at[0], cs.at[1], mate, v)
    half_copy.start()
    half_copy.wait()
    for k in range(4):
        rd[k] = pk[c, k] + rc[k]

    def r_copy(d):
        to = (x + d) % 4
        return copy(rd.at[to], rx.at[d - 1], rs.at[d - 1], rr.at[d - 1], o, 4 * y + to)

    for d in (2, 1, 3):
        r_copy(d).start()
    for d in (1, 2, 3):
        r_copy(d).wait()

    def dot(a, b, dims=(((1,), (0,)), ((), ()))):
        return lax.dot_general(a, b, dims, precision=HIGH, preferred_element_type=F32)

    for p in range(3):
        total = (rd[x, p] + rx[0, p]) + (rx[1, p] + rx[2, p])
        plane = jnp.concatenate(unpack(total, lane), axis=0)
        plane = dot(small[2, :, :96], dot(plane, small[0]))
        x1[:, p] = plane.reshape(16, 8, 128)

    def layer_exchange(src, dst, send, recv):
        def one(d):
            to = (v + d) % 16
            return copy(src.at[to], dst.at[v], send.at[d], recv.at[d], o, to)

        @pl.loop(1, 16)
        def _(d):
            one(d).start()

        dst[v] = src[v]

        @pl.loop(1, 16)
        def _(d):
            one(d).wait()

    layer_exchange(x1, y1, a1s, a1r)

    def column_start(src, dst, send, recv):
        def one(d):
            to = (o + d) % 32
            return copy(src.at[to], dst.at[o], send.at[d], recv.at[d], to, v)

        @pl.loop(1, 32)
        def _(d):
            one(d).start()

        dst[o] = src[o]
        return one

    def column_wait(one):
        @pl.loop(1, 32)
        def _(d):
            one(d).wait()

    for p in range(3):
        flat = y1[:, p].reshape(128, 128)
        u1[:, p] = flat.T.reshape(32, 4, 128)
    first = column_start(u1, w1, b1s, b1r)
    column_wait(first)
    load_kz.wait()
    spectral = dot(kz[...], w1[...].reshape(384, 128)) * damp[...]
    u2[...] = dot(kz[...], spectral).reshape(32, 3, 4, 128)
    second = column_start(u2, w2, b2s, b2r)

    full = dot(spectral, spectral, (((0,), (0,)), ((), ()))) * small[6]
    gram = dot(small[5], dot(full, small[4]))[:16, :]
    slot = 2 * v + c
    t1[slot] = gram[:8] + pltpu.roll(gram[8:], 16, 1)

    def g1_copy(d, other):
        to = (v + d) % 16
        orb = mate if other else o
        return copy(t1.at[slot], t1.at[slot], g1s.at[2 * d + other], g1r.at[2 * d + other], orb, to)

    g1_copy(0, 1).start()

    @pl.loop(1, 16)
    def _(d):
        g1_copy(d, 0).start()
        g1_copy(d, 1).start()

    g1_copy(0, 1).wait()

    @pl.loop(1, 16)
    def _(d):
        g1_copy(d, 0).wait()
        g1_copy(d, 1).wait()

    t2[z] = jnp.sum(t1[...], axis=0)

    def g2_copy(d):
        return copy(t2.at[z], t2.at[z], g2s.at[d], g2r.at[d], 2 * ((z + d) % 16) + c, v)

    @pl.loop(1, 16)
    def _(d):
        g2_copy(d).start()

    @pl.loop(1, 16)
    def _(d):
        g2_copy(d).wait()

    folded = jnp.sum(t2[...], axis=0) * (1.0 / (NZ * NYX))
    row = lax.broadcasted_iota(jnp.int32, (16, 128), 0)
    col = lax.broadcasted_iota(jnp.int32, (16, 128), 1)
    work = jnp.concatenate([folded, pltpu.roll(folded, 112, 1)], axis=0)
    work = jnp.where(col < 16, work, jnp.where(col == row + 16, 1.0, 0.0))

    def eliminate(j, work):
        pivot_row = jnp.sum(jnp.where(row == j, work, 0.0), axis=0, keepdims=True)
        pivot_col = jnp.sum(jnp.where(col == j, work, 0.0), axis=1, keepdims=True)
        pivot = jnp.sum(jnp.where((row == j) & (col == j), work, 0.0), axis=(0, 1), keepdims=True)
        scaled = pivot_row * (1.0 / jnp.sqrt(pivot))
        reduced = work - (pivot_col * (1.0 / pivot)) * pivot_row
        return jnp.where(row == j, scaled, jnp.where(row > j, reduced, work))

    work = lax.fori_loop(0, 16, eliminate, work)
    factor[...] = jnp.where(col >= row, work, 0.0)[:, :16]
    right = pltpu.roll(work, 112, 1)
    right = jnp.where(col < 16, right, 0.0)
    right = jnp.concatenate([right, jnp.zeros((112, 128), F32)], axis=0)
    mix = dot(dot(small[4], right), small[5]) * small[6]

    column_wait(second)
    for p in range(3):
        flat = w2[:, p].reshape(128, 128)
        x2[:, p] = dot(mix, flat, (((1,), (1,)), ((), ()))).reshape(16, 8, 128)
    layer_exchange(x2, y2, a2s, a2r)
    for p in range(3):
        flat = y2[:, p].reshape(128, 128)
        plane = dot(dot(small[3, :96, :], flat), small[1])
        f = pack([plane[24 * s : 24 * s + 24] for s in range(4)], lane)
        for t in range(3):
            out[p, :, 128 * t : 128 * t + 128] = f[t]


def body(orbitals, energies, trial_potential, local_potential):
    o = lax.axis_index("orb")
    v = lax.axis_index("vec")
    z = o // 2
    y, x = v // 4, v % 4
    wanted = []
    for q in range(4):
        to = (z + 16 - offset(x, q)) % 16
        wanted.append(6 * to - 3 + 3 * y)
    at = jnp.concatenate([w + jnp.arange(3) for w in wanted])
    pickz = (at[:, None] == jnp.arange(NZ)[None, :]).astype(BF16)
    pieces = jnp.dot(pickz, orbitals[0], preferred_element_type=F32).astype(BF16)
    psi_in = pieces.reshape(4, 3, 24, 384)
    pert = trial_potential.reshape(3, 24, 384)
    pot = local_potential.reshape(3, 24, 384)
    energy = jnp.broadcast_to(energies.reshape(1, 1), (8, 128))
    i = jnp.arange(128)[None, :] % 8
    r = jnp.arange(384)[:, None]

    def eigen(position):
        return 2.0 - 2.0 * jnp.cos(jnp.pi * (position.astype(F32) + 1.0) / 97)

    denom = (eigen(r // 4) + eigen(6 * v + i)) + eigen(3 * o + r % 4)
    damp = jnp.where((i < 6) & (r % 4 < 3), jnp.sqrt(4.0 * jnp.pi) / jnp.sqrt(denom), 0.0)
    small, kz = tables()
    vmem = pl.BlockSpec(memory_space=pltpu.VMEM)
    dma = pltpu.SemaphoreType.DMA
    piece = (3, 24, 384)
    blocks = (12, 4, 24, 128)
    ortho, factor = pl.pallas_call(
        kernel,
        out_shape=(
            jax.ShapeDtypeStruct(piece, F32),
            jax.ShapeDtypeStruct((16, 16), F32),
        ),
        in_specs=[vmem] * 5 + [pl.BlockSpec(memory_space=pl.ANY), vmem],
        out_specs=(vmem, vmem),
        scratch_shapes=[
            pltpu.VMEM((384, 384), F32),
            pltpu.VMEM((4, 4) + piece, BF16),
            pltpu.VMEM((4, 8, 128), F32),
            pltpu.VMEM((4, 5) + piece, BF16),
            pltpu.VMEM((4,) + blocks, F32),
            pltpu.VMEM(blocks, F32),
            pltpu.VMEM(blocks, F32),
            pltpu.VMEM(blocks, F32),
            pltpu.VMEM(blocks, F32),
            pltpu.VMEM((12, 4, 40, 128), F32),
            pltpu.VMEM((12, 4, 40, 128), F32),
            pltpu.VMEM((12, 4, 40, 128), F32),
            pltpu.VMEM((4, 6, 4, 24, 128), F32),
            pltpu.VMEM((2, 4) + piece, F32),
            pltpu.VMEM((4,) + piece, F32),
            pltpu.VMEM((4,) + piece, F32),
            pltpu.VMEM((3,) + piece, F32),
            pltpu.VMEM((16, 3, 8, 128), F32),
            pltpu.VMEM((16, 3, 8, 128), F32),
            pltpu.VMEM((32, 3, 4, 128), F32),
            pltpu.VMEM((32, 3, 4, 128), F32),
            pltpu.VMEM((32, 3, 4, 128), F32),
            pltpu.VMEM((32, 3, 4, 128), F32),
            pltpu.VMEM((16, 3, 8, 128), F32),
            pltpu.VMEM((16, 3, 8, 128), F32),
            pltpu.VMEM((32, 8, 128), F32),
            pltpu.VMEM((16, 8, 128), F32),
            dma((4,)), dma((4,)), dma((4,)), dma((4,)), dma((3,)), dma((3,)), dma((3,)), dma((3,)),
            dma((12,)), dma((12,)), dma((2,)), dma((3,)), dma((3,)),
            dma((16,)), dma((16,)), dma((32,)), dma((32,)), dma((32,)), dma((32,)),
            dma((32,)), dma((32,)), dma((16,)), dma((16,)), dma((16,)), dma((16,)), dma(()),
        ],
        compiler_params=pltpu.CompilerParams(
            collective_id=0, has_side_effects=True, vmem_limit_bytes=48 << 20
        ),
    )(psi_in, pert, pot, energy, jnp.asarray(small), jnp.asarray(kz), damp)
    return ortho.reshape(1, 3, NYX), factor


def solution(mesh):
    in_specs = (P("orb", None, None), P("orb"), P("vec", "orb", None), P("orb", None))
    out_specs = (P("vec", "orb", None), P())
    return jax.shard_map(body, mesh=mesh, in_specs=in_specs, out_specs=out_specs, check_vma=False)
```

```python
import jax
import jax.numpy as jnp
import numpy as np
from jax import lax
from jax.experimental import pallas as pl
from jax.experimental.pallas import tpu as pltpu
from jax.sharding import PartitionSpec as P

NZ = 96
NY = 96
NX = 96
NYX = 9216
NORB = 32
NV = 16
F32 = jnp.float32
BF16 = jnp.bfloat16
HIGH = lax.Precision.HIGHEST
T4 = 8.0 / 0.8**4 - 8.0 / 0.8**2 + 1.0
Q0 = (T4 - 1.0) / T4
Q2 = (8.0 / 0.8**4) / T4
SCALE = 4.0 / NORB
ZORDER = (0, 2, 1, 3)


def sine(n):
    i = np.arange(n, dtype=np.float64) + 1.0
    return np.sqrt(2.0 / (n + 1)) * np.sin(np.pi * i[:, None] * i[None, :] / (n + 1))


def tables():
    s = sine(96)
    row_y = np.arange(96)
    y_of = 4 * (row_y % 24) + row_y // 24
    sx = np.zeros((128, 128))
    for g in range(32):
        for r in range(3):
            sx[:96, 4 * g + r] = s[:, 3 * g + r]
    sy = np.zeros((128, 128))
    for w in range(16):
        for i in range(6):
            sy[8 * w + i, :96] = s[6 * w + i, y_of]
    kz = np.kron(s, np.eye(4))
    pick = np.zeros((128, 128))
    same = np.zeros((128, 128))
    for a in range(128):
        pick[a, a // 8] = 1.0
        for b in range(128):
            same[a, b] = float(a % 8 == b % 8)
    small = np.stack([sx, sx.T, sy, sy.T, pick, pick.T, same])
    return small.astype(np.float32), kz.astype(np.float32)


def offset(x, q):
    base = 8 * (q % 2)
    if q < 2:
        return base + x
    return (base + 16 - x + jnp.where(x == 0, 4, 0)) % 16


def unpack(packed, lane):
    f0, f1, f2 = packed[:, :128], packed[:, 128:256], packed[:, 256:]
    y0 = jnp.where(lane < 96, f0, 0.0)
    y1 = jnp.where(lane < 32, pltpu.roll(f0, 32, 1), jnp.where(lane < 96, pltpu.roll(f1, 32, 1), 0.0))
    y2 = jnp.where(lane < 64, pltpu.roll(f1, 64, 1), jnp.where(lane < 96, pltpu.roll(f2, 64, 1), 0.0))
    y3 = jnp.where(lane < 96, pltpu.roll(f2, 96, 1), 0.0)
    return y0, y1, y2, y3


def pack(y, lane):
    r1, r2, r3 = pltpu.roll(y[1], 96, 1), pltpu.roll(y[2], 64, 1), pltpu.roll(y[3], 32, 1)
    return (
        jnp.where(lane < 96, y[0], r1),
        jnp.where(lane < 64, r1, r2),
        jnp.where(lane < 32, r2, r3),
    )


def kernel(
    psi_in, pert, pot, energy, small, kz_hbm, damp, out, factor,
    kz, psi_all, en_all, pv, vf, potf, cf, pdf, psif, gf, hf, mf, acc,
    pk, rc, rd, rx, x1, y1, u1, w1, u2, w2, x2, y2, t1, t2,
    zs, zr, es, er, xs, xr, hs, hr, ys, yr, cs, rs, rr,
    a1s, a1r, b1s, b1r, b2s, b2r, g1s, g1r, g2s, g2r, a2s, a2r, ks,
):
    o = lax.axis_index("orb")
    v = lax.axis_index("vec")
    z, c = o // 2, o % 2
    y, x = v // 4, v % 4
    mate = 2 * z + 1 - c

    def copy(src, dst, send, recv, orb, vec):
        return pltpu.make_async_remote_copy(
            src_ref=src, dst_ref=dst, send_sem=send, recv_sem=recv,
            device_id={"orb": orb, "vec": vec}, device_id_type=pl.DeviceIdType.MESH,
        )

    barrier = pltpu.get_barrier_semaphore()

    def greet(orb, vec):
        pl.semaphore_signal(
            barrier, inc=1, device_id={"orb": orb, "vec": vec}, device_id_type=pl.DeviceIdType.MESH
        )

    @pl.loop(1, 32)
    def _(d):
        greet((o + d) % 32, v)

    @pl.loop(1, 16)
    def _(d):
        greet(o, (v + d) % 16)
        greet(mate, (v + d) % 16)

    load_kz = pltpu.make_async_copy(kz_hbm, kz, ks)
    load_kz.start()
    own = 1 + c
    pv[own, x] = pert[...]
    pv[own, 4] = pot[...]
    for f in (gf, hf, mf):
        f[:, :, :8, :] = jnp.zeros((12, 4, 8, 128), F32)
        f[:, :, 32:, :] = jnp.zeros((12, 4, 8, 128), F32)
    acc[...] = jnp.zeros(acc.shape, F32)
    pl.semaphore_wait(barrier, 61)

    def z_copy(q):
        return copy(psi_in.at[q], psi_all.at[y, q], zs.at[q], zr.at[q], 2 * ((z + 16 - offset(x, q)) % 16) + c, v)

    def e_copy(q):
        return copy(energy, en_all.at[q], es.at[q], er.at[q], 2 * ((z + 16 - offset(x, q)) % 16) + c, v)

    def x_copy(d):
        return copy(pert, pv.at[own, x], xs.at[d - 1], xr.at[d - 1], o, 4 * y + (x + d) % 4)

    for d in (2, 1, 3):
        x_copy(d).start()

    @pl.when(x != 0)
    def _():
        z_copy(0).start()
        e_copy(0).start()

    @pl.when(x == 0)
    def _():
        psi_all[y, 0] = psi_in[0]
        en_all[0] = energy[...]

    for q in ZORDER[1:]:
        z_copy(q).start()
        e_copy(q).start()

    far = 3 - 3 * c
    h_mate = copy(pv.at[own], pv.at[own], hs.at[0], hr.at[0], mate, v)
    h_next = copy(pv.at[own], pv.at[far], hs.at[1], hr.at[1], 2 * ((z + 2 * c + 15) % 16) + c, v)
    h_pass = copy(pv.at[far], pv.at[far], hs.at[2], hr.at[2], mate, v)
    for d in (1, 2, 3):
        x_copy(d).wait()
    h_next.start()
    h_mate.start()

    def y_copy(q, d):
        return copy(psi_all.at[y, q], psi_all.at[y, q], ys.at[3 * q + d - 1], yr.at[3 * q + d - 1], o, 4 * ((y + d) % 4) + x)

    def spread(q):
        def arrived():
            z_copy(q).wait()
            e_copy(q).wait()

        if q == 0:
            pl.when(x != 0)(arrived)
        else:
            arrived()
        for d in (2, 1, 3):
            y_copy(q, d).start()

    lane = lax.broadcasted_iota(jnp.int32, (24, 128), 1)

    def solve(q):
        for d in (1, 2, 3):
            y_copy(q, d).wait()
        level = en_all[q, 0:1, :]

        @pl.loop(0, 12, unroll=4)
        def _(p):
            plane = 6 * z - 3 + p
            half = jnp.where((plane >= 0) & (plane < NZ), 0.5, 0.0)
            psi = unpack(psi_all[p // 3, q, p % 3].astype(F32), lane)
            for s in range(4):
                inverse = 1.0 / (3.25 + potf[p, s] - level)
                cf[p, s] = jnp.where(lane < 96, half * inverse, 0.0)
                pdf[p, s] = -psi[s] * inverse
                psif[p, s] = psi[s]

        def stencil(f, p):
            mid = [f[p, s, 8:32, :] for s in range(4)]
            total = []
            for s in range(4):
                up = mid[s - 1] if s > 0 else f[p, 3, 7:31, :]
                down = mid[s + 1] if s < 3 else f[p, 0, 9:33, :]
                n = (f[p - 1, s, 8:32, :] + f[p + 1, s, 8:32, :]) + (up + down)
                n = n + (pltpu.roll(mid[s], 1, 1) + pltpu.roll(mid[s], 127, 1))
                total.append(cf[p, s] * n)
            return mid, total

        @pl.loop(0, 4)
        def _(k):
            @pl.loop(0, 12, unroll=12)
            def _(p):
                for s in range(4):
                    gf[p, s, 8:32, :] = vf[k, p, s] * pdf[p, s]

            @pl.loop(1, 11, unroll=10)
            def _(p):
                mid, total = stencil(gf, p)
                for s in range(4):
                    hf[p, s, 8:32, :] = mid[s] + total[s]

            @pl.loop(2, 10, unroll=8)
            def _(p):
                _, total = stencil(hf, p)
                for s in range(4):
                    mf[p, s, 8:32, :] = total[s]

            @pl.loop(3, 9, unroll=6)
            def _(p):
                _, total = stencil(mf, p)
                for s in range(4):
                    answer = (SCALE * Q0) * hf[p, s, 8:32, :] + (SCALE * Q2) * total[s]
                    acc[k, p - 3, s] = acc[k, p - 3, s] + psif[p, s] * answer

    spread(0)
    spread(2)
    h_next.wait()
    h_pass.start()
    h_mate.wait()
    spread(1)
    h_pass.wait()

    @pl.loop(0, 12)
    def _(p):
        slab, t = p // 3, p % 3
        for k in range(4):
            field = unpack(pv[slab, k, t].astype(F32), lane)
            for s in range(4):
                vf[k, p, s] = field[s]
        field = unpack(pv[slab, 4, t].astype(F32), lane)
        for s in range(4):
            potf[p, s] = field[s]

    solve(0)
    spread(3)
    solve(2)
    solve(1)
    solve(3)

    @pl.loop(0, 4)
    def _(k):
        for p in range(6):
            f = pack([acc[k, p, s] for s in range(4)], lane)
            for t in range(3):
                pk[p // 3, k, p % 3, :, 128 * t : 128 * t + 128] = f[t]

    half_copy = copy(pk.at[1 - c], rc, cs.at[0], cs.at[1], mate, v)
    half_copy.start()
    half_copy.wait()
    for k in range(4):
        rd[k] = pk[c, k] + rc[k]

    def r_copy(d):
        to = (x + d) % 4
        return copy(rd.at[to], rx.at[d - 1], rs.at[d - 1], rr.at[d - 1], o, 4 * y + to)

    for d in (2, 1, 3):
        r_copy(d).start()
    for d in (1, 2, 3):
        r_copy(d).wait()

    def dot(a, b, dims=(((1,), (0,)), ((), ()))):
        return lax.dot_general(a, b, dims, precision=HIGH, preferred_element_type=F32)

    for p in range(3):
        total = (rd[x, p] + rx[0, p]) + (rx[1, p] + rx[2, p])
        plane = jnp.concatenate(unpack(total, lane), axis=0)
        plane = dot(small[2, :, :96], dot(plane, small[0]))
        x1[:, p] = plane.reshape(16, 8, 128)

    def layer_exchange(src, dst, send, recv):
        def one(d):
            to = (v + d) % 16
            return copy(src.at[to], dst.at[v], send.at[d], recv.at[d], o, to)

        @pl.loop(1, 16)
        def _(d):
            one(d).start()

        dst[v] = src[v]

        @pl.loop(1, 16)
        def _(d):
            one(d).wait()

    layer_exchange(x1, y1, a1s, a1r)

    def column_start(src, dst, send, recv):
        def one(d):
            to = (o + d) % 32
            return copy(src.at[to], dst.at[o], send.at[d], recv.at[d], to, v)

        @pl.loop(1, 32)
        def _(d):
            one(d).start()

        dst[o] = src[o]
        return one

    def column_wait(one):
        @pl.loop(1, 32)
        def _(d):
            one(d).wait()

    for p in range(3):
        flat = y1[:, p].reshape(128, 128)
        u1[:, p] = flat.T.reshape(32, 4, 128)
    first = column_start(u1, w1, b1s, b1r)
    column_wait(first)
    load_kz.wait()
    spectral = dot(kz[...], w1[...].reshape(384, 128)) * damp[...]
    u2[...] = dot(kz[...], spectral).reshape(32, 3, 4, 128)
    second = column_start(u2, w2, b2s, b2r)

    full = dot(spectral, spectral, (((0,), (0,)), ((), ()))) * small[6]
    gram = dot(small[5], dot(full, small[4]))[:16, :]
    slot = 2 * v + c
    t1[slot] = gram[:8] + pltpu.roll(gram[8:], 16, 1)

    def g1_copy(d, other):
        to = (v + d) % 16
        orb = mate if other else o
        return copy(t1.at[slot], t1.at[slot], g1s.at[2 * d + other], g1r.at[2 * d + other], orb, to)

    g1_copy(0, 1).start()

    @pl.loop(1, 16)
    def _(d):
        g1_copy(d, 0).start()
        g1_copy(d, 1).start()

    g1_copy(0, 1).wait()

    @pl.loop(1, 16)
    def _(d):
        g1_copy(d, 0).wait()
        g1_copy(d, 1).wait()

    t2[z] = jnp.sum(t1[...], axis=0)

    def g2_copy(d):
        return copy(t2.at[z], t2.at[z], g2s.at[d], g2r.at[d], 2 * ((z + d) % 16) + c, v)

    @pl.loop(1, 16)
    def _(d):
        g2_copy(d).start()

    @pl.loop(1, 16)
    def _(d):
        g2_copy(d).wait()

    folded = jnp.sum(t2[...], axis=0) * (1.0 / (NZ * NYX))
    row = lax.broadcasted_iota(jnp.int32, (16, 128), 0)
    col = lax.broadcasted_iota(jnp.int32, (16, 128), 1)
    work = jnp.concatenate([folded, pltpu.roll(folded, 112, 1)], axis=0)
    work = jnp.where(col < 16, work, jnp.where(col == row + 16, 1.0, 0.0))

    def eliminate(j, work):
        pivot_row = jnp.sum(jnp.where(row == j, work, 0.0), axis=0, keepdims=True)
        pivot_col = jnp.sum(jnp.where(col == j, work, 0.0), axis=1, keepdims=True)
        pivot = jnp.sum(jnp.where((row == j) & (col == j), work, 0.0), axis=(0, 1), keepdims=True)
        scaled = pivot_row * (1.0 / jnp.sqrt(pivot))
        reduced = work - (pivot_col * (1.0 / pivot)) * pivot_row
        return jnp.where(row == j, scaled, jnp.where(row > j, reduced, work))

    work = lax.fori_loop(0, 16, eliminate, work)
    factor[...] = jnp.where(col >= row, work, 0.0)[:, :16]
    right = pltpu.roll(work, 112, 1)
    right = jnp.where(col < 16, right, 0.0)
    right = jnp.concatenate([right, jnp.zeros((112, 128), F32)], axis=0)
    mix = dot(dot(small[4], right), small[5]) * small[6]

    column_wait(second)
    for p in range(3):
        flat = w2[:, p].reshape(128, 128)
        x2[:, p] = dot(mix, flat, (((1,), (1,)), ((), ()))).reshape(16, 8, 128)
    layer_exchange(x2, y2, a2s, a2r)
    for p in range(3):
        flat = y2[:, p].reshape(128, 128)
        plane = dot(dot(small[3, :96, :], flat), small[1])
        f = pack([plane[24 * s : 24 * s + 24] for s in range(4)], lane)
        for t in range(3):
            out[p, :, 128 * t : 128 * t + 128] = f[t]


def body(orbitals, energies, trial_potential, local_potential):
    o = lax.axis_index("orb")
    v = lax.axis_index("vec")
    z = o // 2
    y, x = v // 4, v % 4
    wanted = []
    for q in range(4):
        to = (z + 16 - offset(x, q)) % 16
        wanted.append(6 * to - 3 + 3 * y)
    at = jnp.concatenate([w + jnp.arange(3) for w in wanted])
    pickz = (at[:, None] == jnp.arange(NZ)[None, :]).astype(BF16)
    pieces = jnp.dot(pickz, orbitals[0], preferred_element_type=F32).astype(BF16)
    psi_in = pieces.reshape(4, 3, 24, 384)
    pert = trial_potential.reshape(3, 24, 384)
    pot = local_potential.reshape(3, 24, 384)
    energy = jnp.broadcast_to(energies.reshape(1, 1), (8, 128))
    i = jnp.arange(128)[None, :] % 8
    r = jnp.arange(384)[:, None]

    def eigen(position):
        return 2.0 - 2.0 * jnp.cos(jnp.pi * (position.astype(F32) + 1.0) / 97)

    denom = (eigen(r // 4) + eigen(6 * v + i)) + eigen(3 * o + r % 4)
    damp = jnp.where((i < 6) & (r % 4 < 3), jnp.sqrt(4.0 * jnp.pi) / jnp.sqrt(denom), 0.0)
    small, kz = tables()
    vmem = pl.BlockSpec(memory_space=pltpu.VMEM)
    dma = pltpu.SemaphoreType.DMA
    piece = (3, 24, 384)
    blocks = (12, 4, 24, 128)
    ortho, factor = pl.pallas_call(
        kernel,
        out_shape=(
            jax.ShapeDtypeStruct(piece, F32),
            jax.ShapeDtypeStruct((16, 16), F32),
        ),
        in_specs=[vmem] * 5 + [pl.BlockSpec(memory_space=pl.ANY), vmem],
        out_specs=(vmem, vmem),
        scratch_shapes=[
            pltpu.VMEM((384, 384), F32),
            pltpu.VMEM((4, 4) + piece, BF16),
            pltpu.VMEM((4, 8, 128), F32),
            pltpu.VMEM((4, 5) + piece, BF16),
            pltpu.VMEM((4,) + blocks, F32),
            pltpu.VMEM(blocks, F32),
            pltpu.VMEM(blocks, F32),
            pltpu.VMEM(blocks, F32),
            pltpu.VMEM(blocks, F32),
            pltpu.VMEM((12, 4, 40, 128), F32),
            pltpu.VMEM((12, 4, 40, 128), F32),
            pltpu.VMEM((12, 4, 40, 128), F32),
            pltpu.VMEM((4, 6, 4, 24, 128), F32),
            pltpu.VMEM((2, 4) + piece, F32),
            pltpu.VMEM((4,) + piece, F32),
            pltpu.VMEM((4,) + piece, F32),
            pltpu.VMEM((3,) + piece, F32),
            pltpu.VMEM((16, 3, 8, 128), F32),
            pltpu.VMEM((16, 3, 8, 128), F32),
            pltpu.VMEM((32, 3, 4, 128), F32),
            pltpu.VMEM((32, 3, 4, 128), F32),
            pltpu.VMEM((32, 3, 4, 128), F32),
            pltpu.VMEM((32, 3, 4, 128), F32),
            pltpu.VMEM((16, 3, 8, 128), F32),
            pltpu.VMEM((16, 3, 8, 128), F32),
            pltpu.VMEM((32, 8, 128), F32),
            pltpu.VMEM((16, 8, 128), F32),
            dma((4,)), dma((4,)), dma((4,)), dma((4,)), dma((3,)), dma((3,)), dma((3,)), dma((3,)),
            dma((12,)), dma((12,)), dma((2,)), dma((3,)), dma((3,)),
            dma((16,)), dma((16,)), dma((32,)), dma((32,)), dma((32,)), dma((32,)),
            dma((32,)), dma((32,)), dma((16,)), dma((16,)), dma((16,)), dma((16,)), dma(()),
        ],
        compiler_params=pltpu.CompilerParams(
            collective_id=0, has_side_effects=True, vmem_limit_bytes=48 << 20
        ),
    )(psi_in, pert, pot, energy, jnp.asarray(small), jnp.asarray(kz), damp)
    return ortho.reshape(1, 3, NYX), factor


def solution(mesh):
    in_specs = (P("orb", None, None), P("orb"), P("vec", "orb", None), P("orb", None))
    out_specs = (P("vec", "orb", None), P())
    return jax.shard_map(body, mesh=mesh, in_specs=in_specs, out_specs=out_specs, check_vma=False)
```

```python
import jax
import jax.numpy as jnp
import numpy as np
from jax import lax
from jax.experimental import pallas as pl
from jax.experimental.pallas import tpu as pltpu
from jax.sharding import PartitionSpec as P

NZ = 96
NY = 96
NX = 96
NYX = 9216
NORB = 32
NV = 16
F32 = jnp.float32
BF16 = jnp.bfloat16
HIGH = lax.Precision.HIGHEST
T4 = 8.0 / 0.8**4 - 8.0 / 0.8**2 + 1.0
Q0 = (T4 - 1.0) / T4
Q2 = (8.0 / 0.8**4) / T4
SCALE = 4.0 / NORB
ZORDER = (0, 2, 1, 3)


def sine(n):
    i = np.arange(n, dtype=np.float64) + 1.0
    return np.sqrt(2.0 / (n + 1)) * np.sin(np.pi * i[:, None] * i[None, :] / (n + 1))


def tables():
    s = sine(96)
    row_y = np.arange(96)
    y_of = 4 * (row_y % 24) + row_y // 24
    sx = np.zeros((2, 128, 128))
    a, b, e = np.zeros((3, 96, 4, 32, 4))
    for g in range(32):
        for r in range(3):
            sx[0, :96, 4 * g + r] = s[:, 3 * g + r]
            sx[1, :96, 4 * g + (3, 2, 0)[r]] = s[:, 3 * g + r]
            a[:, r, g, r] = s[:, 3 * g]
            b[:, r, g, r] = s[:, 3 * g + 1]
            e[:, 2, g, r] = s[:, 3 * g + 2]
        a[:, 0, g, 3] = s[:, 3 * g + 2]
        b[:, 1, g, 3] = s[:, 3 * g + 2]
    sy = np.zeros((128, 128))
    for w in range(16):
        for i in range(6):
            sy[8 * w + i, :96] = s[6 * w + i, y_of]
    pick = np.zeros((128, 128))
    pick[np.arange(128), np.arange(128) // 8] = 1.0
    small = np.stack([sx[0], sx[1], sy, sy.T, pick])
    kz = np.concatenate([m.reshape(384, 128) for m in (a, b, e)], axis=1)
    return small.astype(np.float32), np.stack([kz, kz.T]).astype(np.float32)


def offset(x, q):
    base = 8 * (q % 2)
    if q < 2:
        return base + x
    return (base + 16 - x + jnp.where(x == 0, 4, 0)) % 16


def unpack(packed, lane):
    f0, f1, f2 = packed[:, :128], packed[:, 128:256], packed[:, 256:]
    y0 = jnp.where(lane < 96, f0, 0.0)
    y1 = jnp.where(lane < 32, pltpu.roll(f0, 32, 1), jnp.where(lane < 96, pltpu.roll(f1, 32, 1), 0.0))
    y2 = jnp.where(lane < 64, pltpu.roll(f1, 64, 1), jnp.where(lane < 96, pltpu.roll(f2, 64, 1), 0.0))
    y3 = jnp.where(lane < 96, pltpu.roll(f2, 96, 1), 0.0)
    return y0, y1, y2, y3


def pack(y, lane):
    r1, r2, r3 = pltpu.roll(y[1], 96, 1), pltpu.roll(y[2], 64, 1), pltpu.roll(y[3], 32, 1)
    return (
        jnp.where(lane < 96, y[0], r1),
        jnp.where(lane < 64, r1, r2),
        jnp.where(lane < 32, r2, r3),
    )


def kernel(
    psi_in, pert, pot, level_ref, small_hbm, kz_hbm, out, factor,
    small, kz, damp, energy, psi_all, en_all, pv, vf, potf, cf, pdf, psif, gf, hf, mf, acc,
    pk, rc, rd, rx, x1, y1, u1, w1, u2, w2, x2, y2, t1, t2,
    zs, zr, es, er, xs, xr, ns, nr, fs, fr, hs, hr, ys, yr, cs, cr, rs, rr,
    a1s, a1r, b1s, b1r, b2s, b2r, g1s, g1r, g2s, g2r, a2s, a2r, ks,
):
    o = lax.axis_index("orb")
    v = lax.axis_index("vec")
    z, c = o // 2, o % 2
    y, x = v // 4, v % 4
    mate = 2 * z + 1 - c

    def copy(src, dst, send, recv, orb, vec):
        return pltpu.make_async_remote_copy(
            src_ref=src, dst_ref=dst, send_sem=send, recv_sem=recv,
            device_id={"orb": orb, "vec": vec}, device_id_type=pl.DeviceIdType.MESH,
        )

    barrier = pltpu.get_barrier_semaphore()

    def greet(orb, vec):
        pl.semaphore_signal(
            barrier, inc=1, device_id={"orb": orb, "vec": vec}, device_id_type=pl.DeviceIdType.MESH
        )

    @pl.loop(1, 32)
    def _(d):
        greet((o + d) % 32, v)

    @pl.loop(1, 16)
    def _(d):
        greet(o, (v + d) % 16)
        greet(mate, (v + d) % 16)

    load_small = pltpu.make_async_copy(small_hbm, small, ks.at[0])
    load_kz = pltpu.make_async_copy(kz_hbm, kz, ks.at[1])
    load_small.start()
    load_kz.start()
    energy[...] = jnp.broadcast_to(level_ref[...], (8, 128))
    own = 1 + c
    pv[own, x] = pert[...]
    pv[own, 4] = pot[...]
    for f in (gf, hf, mf):
        f[:, :, :8, :] = jnp.zeros((12, 4, 8, 128), F32)
        f[:, :, 32:, :] = jnp.zeros((12, 4, 8, 128), F32)
    acc[...] = jnp.zeros(acc.shape, F32)

    def eigen(position):
        return 2.0 - 2.0 * jnp.cos(jnp.pi * (position.astype(F32) + 1.0) / 97)

    r8 = lax.broadcasted_iota(jnp.int32, (8, 128), 0)
    i8 = lax.broadcasted_iota(jnp.int32, (8, 128), 1) % 8
    plane_part = eigen(6 * v + i8) + eigen(3 * o + r8 % 4)
    kept = (i8 < 6) & (r8 % 4 < 3)
    for n in range(48):
        denom = eigen(2 * n + r8 // 4) + plane_part
        damp[8 * n : 8 * n + 8, :] = jnp.where(kept, jnp.sqrt(4.0 * jnp.pi) / jnp.sqrt(denom), 0.0)
    pl.semaphore_wait(barrier, 61)

    def z_copy(q):
        return copy(psi_in.at[q], psi_all.at[y, q], zs.at[q], zr.at[q], 2 * ((z + 16 - offset(x, q)) % 16) + c, v)

    def e_copy(q):
        return copy(energy, en_all.at[q], es.at[q], er.at[q], 2 * ((z + 16 - offset(x, q)) % 16) + c, v)

    def x_copy(d):
        return copy(pert, pv.at[own, x], xs.at[d - 1], xr.at[d - 1], o, 4 * y + (x + d) % 4)

    far = 3 - 3 * c
    next_orb = 2 * ((z + 2 * c + 15) % 16) + c

    def n_copy(k):
        return copy((pert, pot)[k], pv.at[far, (x, 4)[k]], ns.at[k], nr.at[k], next_orb, v)

    def f_copy(d):
        return copy(pv.at[far, x], pv.at[far, x], fs.at[d - 1], fr.at[d - 1], o, 4 * y + (x + d) % 4)

    def h_copy(k):
        slab = (own, far)[k]
        return copy(pv.at[slab], pv.at[slab], hs.at[k], hr.at[k], mate, v)

    n_copy(0).start()
    n_copy(1).start()
    for d in (2, 1, 3):
        x_copy(d).start()

    @pl.when(x != 0)
    def _():
        z_copy(0).start()
        e_copy(0).start()

    @pl.when(x == 0)
    def _():
        psi_all[y, 0] = psi_in[0]
        en_all[0] = energy[...]

    for q in ZORDER[1:]:
        z_copy(q).start()
        e_copy(q).start()

    def y_copy(q, d):
        return copy(psi_all.at[y, q], psi_all.at[y, q], ys.at[3 * q + d - 1], yr.at[3 * q + d - 1], o, 4 * ((y + d) % 4) + x)

    def spread(q):
        def arrived():
            z_copy(q).wait()
            e_copy(q).wait()

        if q == 0:
            pl.when(x != 0)(arrived)
        else:
            arrived()
        for d in (2, 1, 3):
            y_copy(q, d).start()

    lane = lax.broadcasted_iota(jnp.int32, (24, 128), 1)

    def vector(n):
        return (x + jnp.where(n == 0, 2, jnp.where(n == 1, 1, jnp.where(n == 2, 3, 0)))) % 4

    def half_copy(n):
        return copy(pk.at[1 - c, vector(n)], rc.at[vector(n)], cs.at[n], cr.at[n], mate, v)

    def r_copy(n):
        return copy(rd.at[vector(n)], rx.at[n], rs.at[n], rr.at[n], o, 4 * y + vector(n))

    def finish(n):
        half_copy(n).wait()
        rd[vector(n)] = pk[c, vector(n)] + rc[vector(n)]

    def reduce(n):
        k = vector(n)
        for p in range(6):
            f = pack([acc[k, p, s] for s in range(4)], lane)
            for t in range(3):
                pk[p // 3, k, p % 3, :, 128 * t : 128 * t + 128] = f[t]
        half_copy(n).start()

        @pl.when(n > 0)
        def _():
            finish(n - 1)
            r_copy(n - 1).start()

    def solve(q, after):
        for d in (1, 2, 3):
            y_copy(q, d).wait()
        level = en_all[q, 0:1, :]

        @pl.loop(0, 12, unroll=4)
        def _(p):
            plane = 6 * z - 3 + p
            half = jnp.where((plane >= 0) & (plane < NZ), 0.5, 0.0)
            psi = unpack(psi_all[p // 3, q, p % 3].astype(F32), lane)
            for s in range(4):
                inverse = 1.0 / (3.25 + potf[p, s] - level)
                cf[p, s] = jnp.where(lane < 96, half * inverse, 0.0)
                pdf[p, s] = -psi[s] * inverse
                psif[p, s] = psi[s]

        def stencil(f, p):
            mid = [f[p, s, 8:32, :] for s in range(4)]
            total = []
            for s in range(4):
                up = mid[s - 1] if s > 0 else f[p, 3, 7:31, :]
                down = mid[s + 1] if s < 3 else f[p, 0, 9:33, :]
                n = (f[p - 1, s, 8:32, :] + f[p + 1, s, 8:32, :]) + (up + down)
                n = n + (pltpu.roll(mid[s], 1, 1) + pltpu.roll(mid[s], 127, 1))
                total.append(cf[p, s] * n)
            return mid, total

        @pl.loop(0, 4)
        def _(n):
            k = vector(n)

            @pl.loop(0, 12, unroll=12)
            def _(p):
                for s in range(4):
                    gf[p, s, 8:32, :] = vf[k, p, s] * pdf[p, s]

            @pl.loop(1, 11, unroll=10)
            def _(p):
                mid, total = stencil(gf, p)
                for s in range(4):
                    hf[p, s, 8:32, :] = mid[s] + total[s]

            @pl.loop(2, 10, unroll=8)
            def _(p):
                _, total = stencil(hf, p)
                for s in range(4):
                    mf[p, s, 8:32, :] = total[s]

            @pl.loop(3, 9, unroll=6)
            def _(p):
                _, total = stencil(mf, p)
                for s in range(4):
                    answer = (SCALE * Q0) * hf[p, s, 8:32, :] + (SCALE * Q2) * total[s]
                    acc[k, p - 3, s] = acc[k, p - 3, s] + psif[p, s] * answer

            if after is not None:
                after(n)

    def widen(slab):
        @pl.loop(0, 3)
        def _(n):
            p = 3 * slab + n
            for k in range(5):
                field = unpack(pv[slab, k, n].astype(F32), lane)
                for s in range(4):
                    if k < 4:
                        vf[k, p, s] = field[s]
                    else:
                        potf[p, s] = field[s]

    n_copy(0).wait()
    n_copy(1).wait()
    for d in (2, 1, 3):
        f_copy(d).start()
    for d in (1, 2, 3):
        x_copy(d).wait()
    h_copy(0).start()
    widen(own)
    for d in (1, 2, 3):
        f_copy(d).wait()
    h_copy(1).start()
    spread(0)
    widen(far)
    spread(2)
    h_copy(0).wait()
    widen(2 - c)
    h_copy(1).wait()
    widen(3 * c)
    spread(1)
    solve(0, None)
    spread(3)
    solve(2, None)
    solve(1, None)
    solve(3, reduce)
    finish(3)
    for n in range(3):
        r_copy(n).wait()

    def dot(a, b, dims=(((1,), (0,)), ((), ()))):
        return lax.dot_general(a, b, dims, precision=HIGH, preferred_element_type=F32)

    load_small.wait()
    load_kz.wait()
    for p in range(3):
        total = (rd[x, p] + rx[0, p]) + (rx[1, p] + rx[2, p])
        plane = jnp.concatenate(unpack(total, lane), axis=0)
        plane = dot(small[2, :, :96], dot(plane, small[p // 2]))
        x1[:, p] = plane.reshape(16, 8, 128)

    def layer_exchange(src, dst, send, recv):
        def one(d):
            to = (v + d) % 16
            return copy(src.at[to], dst.at[v], send.at[d], recv.at[d], o, to)

        @pl.loop(1, 16)
        def _(d):
            one(d).start()

        dst[v] = src[v]

        @pl.loop(1, 16)
        def _(d):
            one(d).wait()

    layer_exchange(x1, y1, a1s, a1r)

    def column_start(src, dst, send, recv):
        def one(d):
            to = (o + d) % 32
            return copy(src.at[to], dst.at[o], send.at[d], recv.at[d], to, v)

        @pl.loop(1, 32)
        def _(d):
            one(d).start()

        dst[o] = src[o]
        return one

    def column_wait(one):
        @pl.loop(1, 32)
        def _(d):
            one(d).wait()

    big = (128, 128)
    slot = lax.broadcasted_iota(jnp.int32, big, 0) % 4
    lanes = lax.broadcasted_iota(jnp.int32, big, 1)
    i = lanes % 8
    across = (((1,), (1,)), ((), ()))
    same = lax.broadcasted_iota(jnp.int32, big, 0) % 8 == i

    def spare(f0, f1, f2):
        moved = jnp.where(slot == 1, pltpu.roll(f1, 4, 1), jnp.where(slot == 2, pltpu.roll(f2, 2, 1), 0.0))
        moved = jnp.where(slot == 0, pltpu.roll(f0, 6, 1), moved)
        return jnp.where(i >= 6, moved, 0.0)

    p0, p1, p2 = [y1[:, p].reshape(big).T for p in range(3)]
    up1, up2 = pltpu.roll(p2, 1, 0), pltpu.roll(p2, 2, 0)
    u1[:, 0] = (p0 + jnp.where(slot == 3, p2, 0.0) + spare(p2, up1, up2)).reshape(32, 4, 128)
    u1[:, 1] = (p1 + jnp.where(slot == 3, up1, 0.0)).reshape(32, 4, 128)
    first = column_start(u1, w1, b1s, b1r)
    column_wait(first)
    half_a, half_b = w1[:, 0].reshape(big), w1[:, 1].reshape(big)
    back = jnp.where((slot == 1) & (i >= 2) & (i < 4), pltpu.roll(half_a, 124, 1), 0.0)
    back = jnp.where((slot == 2) & (i >= 4) & (i < 6), pltpu.roll(half_a, 126, 1), back)
    back = jnp.where((slot == 0) & (i < 2), pltpu.roll(half_a, 122, 1), back)
    spectral = dot(kz[0], jnp.concatenate([half_a, half_b, back], axis=0)) * damp[...]

    full = dot(spectral, spectral, (((0,), (0,)), ((), ())))
    full = jnp.sum(jnp.where(same, full, 0.0).reshape(16, 8, 128), axis=1)
    gram = dot(full, small[4])
    mine = 2 * v + c
    t1[mine] = gram[:8] + pltpu.roll(gram[8:], 16, 1)

    def g1_copy(d, other):
        to = (v + d) % 16
        orb = mate if other else o
        return copy(t1.at[mine], t1.at[mine], g1s.at[2 * d + other], g1r.at[2 * d + other], orb, to)

    g1_copy(0, 1).start()

    @pl.loop(1, 16)
    def _(d):
        g1_copy(d, 0).start()
        g1_copy(d, 1).start()

    columns = dot(kz[1], spectral)
    extra = columns[256:]
    u2[:, 0] = (columns[:128] + spare(extra, extra, extra)).reshape(32, 4, 128)
    u2[:, 1] = columns[128:256].reshape(32, 4, 128)
    second = column_start(u2, w2, b2s, b2r)
    g1_copy(0, 1).wait()

    @pl.loop(1, 16)
    def _(d):
        g1_copy(d, 0).wait()
        g1_copy(d, 1).wait()

    t2[z] = jnp.sum(t1[...], axis=0)

    def g2_copy(d):
        return copy(t2.at[z], t2.at[z], g2s.at[d], g2r.at[d], 2 * ((z + d) % 16) + c, v)

    @pl.loop(1, 16)
    def _(d):
        g2_copy(d).start()

    @pl.loop(1, 16)
    def _(d):
        g2_copy(d).wait()

    folded = jnp.sum(t2[...], axis=0) * (1.0 / (NZ * NYX))
    row = lax.broadcasted_iota(jnp.int32, (16, 128), 0)
    col = lax.broadcasted_iota(jnp.int32, (16, 128), 1)
    work = jnp.concatenate([folded, pltpu.roll(folded, 112, 1)], axis=0)
    work = jnp.where(col < 16, work, jnp.where(col == row + 16, 1.0, 0.0))

    for j in range(15):
        column = jnp.broadcast_to(work[:, j : j + 1], (16, 128))
        ratio = work[j : j + 1, :] * (1.0 / column[j : j + 1, :])
        work = work - jnp.where(row > j, column, 0.0) * ratio
    pivots = jnp.sum(jnp.where(col == row, work, 0.0), axis=1, keepdims=True)
    work = work * (1.0 / jnp.sqrt(pivots))
    factor[...] = jnp.where(col >= row, work, 0.0)[:, :16]
    right = jnp.where(col < 16, pltpu.roll(work, 112, 1), 0.0)
    right = dot(right, small[4], across)
    mix = jnp.broadcast_to(right[:, None, :], (16, 8, 128)).reshape(big)
    mix = jnp.where(same, mix, 0.0)

    column_wait(second)
    half_a, half_b = w2[:, 0].reshape(big), w2[:, 1].reshape(big)
    back = jnp.where(i < 4, pltpu.roll(pltpu.roll(half_a, 127, 0), 124, 1), pltpu.roll(pltpu.roll(half_a, 126, 0), 126, 1))
    back = jnp.where(i < 2, pltpu.roll(half_a, 122, 1), back)
    third = jnp.where(slot == 3, half_a, jnp.where(slot == 2, pltpu.roll(half_b, 127, 0), 0.0))
    third = jnp.where(slot == 0, jnp.where(i < 6, back, 0.0), third)
    for p, plane in enumerate((half_a, half_b, third)):
        x2[:, p] = dot(mix, plane, across).reshape(16, 8, 128)
    layer_exchange(x2, y2, a2s, a2r)
    for p in range(3):
        flat = y2[:, p].reshape(128, 128)
        plane = dot(dot(small[3, :96, :], flat), small[p // 2], across)
        f = pack([plane[24 * s : 24 * s + 24] for s in range(4)], lane)
        for t in range(3):
            out[p, :, 128 * t : 128 * t + 128] = f[t]


def body(orbitals, energies, trial_potential, local_potential):
    o = lax.axis_index("orb")
    v = lax.axis_index("vec")
    z = o // 2
    y, x = v // 4, v % 4
    wanted = []
    for q in range(4):
        to = (z + 16 - offset(x, q)) % 16
        wanted.append(6 * to - 3 + 3 * y)
    at = jnp.concatenate([w + jnp.arange(3) for w in wanted])
    pickz = (at[:, None] == jnp.arange(NZ)[None, :]).astype(BF16)
    pieces = jnp.dot(pickz, orbitals[0], preferred_element_type=F32).astype(BF16)
    psi_in = pieces.reshape(4, 3, 24, 384)
    pert = trial_potential.reshape(3, 24, 384)
    pot = local_potential.reshape(3, 24, 384)
    small, kz = tables()
    vmem = pl.BlockSpec(memory_space=pltpu.VMEM)
    dma = pltpu.SemaphoreType.DMA
    piece = (3, 24, 384)
    blocks = (12, 4, 24, 128)
    ortho, factor = pl.pallas_call(
        kernel,
        out_shape=(
            jax.ShapeDtypeStruct(piece, F32),
            jax.ShapeDtypeStruct((16, 16), F32),
        ),
        in_specs=[vmem] * 4 + [pl.BlockSpec(memory_space=pltpu.HBM)] * 2,
        out_specs=(vmem, vmem),
        scratch_shapes=[
            pltpu.VMEM((5, 128, 128), F32),
            pltpu.VMEM((2, 384, 384), F32),
            pltpu.VMEM((384, 128), F32),
            pltpu.VMEM((8, 128), F32),
            pltpu.VMEM((4, 4) + piece, BF16),
            pltpu.VMEM((4, 8, 128), F32),
            pltpu.VMEM((4, 5) + piece, BF16),
            pltpu.VMEM((4,) + blocks, F32),
            pltpu.VMEM(blocks, F32),
            pltpu.VMEM(blocks, F32),
            pltpu.VMEM(blocks, F32),
            pltpu.VMEM(blocks, F32),
            pltpu.VMEM((12, 4, 40, 128), F32),
            pltpu.VMEM((12, 4, 40, 128), F32),
            pltpu.VMEM((12, 4, 40, 128), F32),
            pltpu.VMEM((4, 6, 4, 24, 128), F32),
            pltpu.VMEM((2, 4) + piece, F32),
            pltpu.VMEM((4,) + piece, F32),
            pltpu.VMEM((4,) + piece, F32),
            pltpu.VMEM((3,) + piece, F32),
            pltpu.VMEM((16, 3, 8, 128), F32),
            pltpu.VMEM((16, 3, 8, 128), F32),
            pltpu.VMEM((32, 2, 4, 128), F32),
            pltpu.VMEM((32, 2, 4, 128), F32),
            pltpu.VMEM((32, 2, 4, 128), F32),
            pltpu.VMEM((32, 2, 4, 128), F32),
            pltpu.VMEM((16, 3, 8, 128), F32),
            pltpu.VMEM((16, 3, 8, 128), F32),
            pltpu.VMEM((32, 8, 128), F32),
            pltpu.VMEM((16, 8, 128), F32),
            dma((4,)), dma((4,)), dma((4,)), dma((4,)), dma((3,)), dma((3,)), dma((2,)), dma((2,)), dma((3,)), dma((3,)), dma((2,)), dma((2,)),
            dma((12,)), dma((12,)), dma((4,)), dma((4,)), dma((3,)), dma((3,)),
            dma((16,)), dma((16,)), dma((32,)), dma((32,)), dma((32,)), dma((32,)),
            dma((32,)), dma((32,)), dma((16,)), dma((16,)), dma((16,)), dma((16,)), dma((2,)),
        ],
        compiler_params=pltpu.CompilerParams(
            collective_id=0, has_side_effects=True, vmem_limit_bytes=48 << 20
        ),
    )(psi_in, pert, pot, energies.reshape(1, 1), jnp.asarray(small), jnp.asarray(kz))
    return ortho.reshape(1, 3, NYX), factor


def solution(mesh):
    in_specs = (P("orb", None, None), P("orb"), P("vec", "orb", None), P("orb", None))
    out_specs = (P("vec", "orb", None), P())
    return jax.shard_map(body, mesh=mesh, in_specs=in_specs, out_specs=out_specs, check_vma=False)
```

```python
import jax
import jax.numpy as jnp
import numpy as np
from jax import lax
from jax.experimental import pallas as pl
from jax.experimental.pallas import tpu as pltpu
from jax.sharding import PartitionSpec as P

NZ = 96
NY = 96
NX = 96
NYX = 9216
NORB = 32
NV = 16
F32 = jnp.float32
BF16 = jnp.bfloat16
T4 = 8.0 / 0.8**4 - 8.0 / 0.8**2 + 1.0
Q0 = (T4 - 1.0) / T4
Q2 = (8.0 / 0.8**4) / T4
SCALE = 4.0 / NORB
ZORDER = (0, 2, 1, 3)


def sine(n):
    i = np.arange(n, dtype=np.float64) + 1.0
    return np.sqrt(2.0 / (n + 1)) * np.sin(np.pi * i[:, None] * i[None, :] / (n + 1))


def tables():
    s = sine(96)
    row_y = np.arange(96)
    y_of = 4 * (row_y % 24) + row_y // 24
    sx = np.zeros((2, 128, 128))
    a, b, e = np.zeros((3, 96, 4, 32, 4))
    for g in range(32):
        for r in range(3):
            sx[0, :96, 4 * g + r] = s[:, 3 * g + r]
            sx[1, :96, 4 * g + (3, 2, 0)[r]] = s[:, 3 * g + r]
            a[:, r, g, r] = s[:, 3 * g]
            b[:, r, g, r] = s[:, 3 * g + 1]
            e[:, 2, g, r] = s[:, 3 * g + 2]
        a[:, 0, g, 3] = s[:, 3 * g + 2]
        b[:, 1, g, 3] = s[:, 3 * g + 2]
    sy = np.zeros((128, 128))
    for w in range(16):
        for i in range(6):
            sy[8 * w + i, :96] = s[6 * w + i, y_of]
    pick = np.zeros((128, 128))
    pick[np.arange(128), np.arange(128) // 8] = 1.0
    small = np.stack([sx[0], sx[1], sy, sy.T, pick])
    kz = np.concatenate([m.reshape(384, 128) for m in (a, b, e)], axis=1)
    kz_high = kz.astype(BF16)
    kz_low = (kz - kz_high.astype(np.float64)).astype(BF16)
    return small.astype(np.float32), np.stack([kz_high, kz_low, kz_high.T, kz_low.T])


def offset(x, q):
    base = 8 * (q % 2)
    if q < 2:
        return base + x
    return (base + 16 - x + jnp.where(x == 0, 4, 0)) % 16


def unpack(packed, lane):
    f0, f1, f2 = packed[:, :128], packed[:, 128:256], packed[:, 256:]
    y0 = jnp.where(lane < 96, f0, 0.0)
    y1 = jnp.where(lane < 32, pltpu.roll(f0, 32, 1), jnp.where(lane < 96, pltpu.roll(f1, 32, 1), 0.0))
    y2 = jnp.where(lane < 64, pltpu.roll(f1, 64, 1), jnp.where(lane < 96, pltpu.roll(f2, 64, 1), 0.0))
    y3 = jnp.where(lane < 96, pltpu.roll(f2, 96, 1), 0.0)
    return y0, y1, y2, y3


def pack(y, lane):
    r1, r2, r3 = pltpu.roll(y[1], 96, 1), pltpu.roll(y[2], 64, 1), pltpu.roll(y[3], 32, 1)
    return (
        jnp.where(lane < 96, y[0], r1),
        jnp.where(lane < 64, r1, r2),
        jnp.where(lane < 32, r2, r3),
    )


def kernel(
    psi_in, pert, pot, level_ref, small_hbm, kz_hbm, out, factor,
    small, kz, damp, energy, psi_all, en_all, pv, vf, potf, cf, pdf, psif, gf, hf, mf, acc,
    pk, rc, rd, rx, x1, y1, u1, w1, u2, w2, x2, y2, t1, t2,
    zs, zr, es, er, xs, xr, ns, nr, fs, fr, hs, hr, ys, yr, cs, cr, rs, rr,
    a1s, a1r, b1s, b1r, b2s, b2r, g1s, g1r, g2s, g2r, a2s, a2r, ks,
):
    o = lax.axis_index("orb")
    v = lax.axis_index("vec")
    z, c = o // 2, o % 2
    y, x = v // 4, v % 4
    mate = 2 * z + 1 - c

    def copy(src, dst, send, recv, orb, vec):
        return pltpu.make_async_remote_copy(
            src_ref=src, dst_ref=dst, send_sem=send, recv_sem=recv,
            device_id={"orb": orb, "vec": vec}, device_id_type=pl.DeviceIdType.MESH,
        )

    barrier = pltpu.get_barrier_semaphore()

    def greet(orb, vec):
        pl.semaphore_signal(
            barrier, inc=1, device_id={"orb": orb, "vec": vec}, device_id_type=pl.DeviceIdType.MESH
        )

    @pl.loop(1, 32)
    def _(d):
        greet((o + d) % 32, v)

    @pl.loop(1, 16)
    def _(d):
        greet(o, (v + d) % 16)
        greet(mate, (v + d) % 16)

    load_small = pltpu.make_async_copy(small_hbm, small, ks.at[0])
    load_kz = pltpu.make_async_copy(kz_hbm, kz, ks.at[1])
    load_small.start()
    load_kz.start()
    energy[...] = jnp.broadcast_to(level_ref[...], (8, 128))
    own = 1 + c
    pv[own, x] = pert[...]
    pv[own, 4] = pot[...]
    for f in (gf, hf, mf):
        f[:, :, :8, :] = jnp.zeros((12, 4, 8, 128), F32)
        f[:, :, 32:, :] = jnp.zeros((12, 4, 8, 128), F32)
    acc[...] = jnp.zeros(acc.shape, F32)

    def eigen(position):
        return 2.0 - 2.0 * jnp.cos(jnp.pi * (position.astype(F32) + 1.0) / 97)

    r8 = lax.broadcasted_iota(jnp.int32, (8, 128), 0)
    i8 = lax.broadcasted_iota(jnp.int32, (8, 128), 1) % 8
    plane_part = eigen(6 * v + i8) + eigen(3 * o + r8 % 4)
    kept = (i8 < 6) & (r8 % 4 < 3)
    for n in range(48):
        denom = eigen(2 * n + r8 // 4) + plane_part
        damp[8 * n : 8 * n + 8, :] = jnp.where(kept, jnp.sqrt(4.0 * jnp.pi) / jnp.sqrt(denom), 0.0)
    pl.semaphore_wait(barrier, 61)

    def z_copy(q):
        return copy(psi_in.at[q], psi_all.at[y, q], zs.at[q], zr.at[q], 2 * ((z + 16 - offset(x, q)) % 16) + c, v)

    def e_copy(q):
        return copy(energy, en_all.at[q], es.at[q], er.at[q], 2 * ((z + 16 - offset(x, q)) % 16) + c, v)

    def x_copy(d):
        return copy(pert, pv.at[own, x], xs.at[d - 1], xr.at[d - 1], o, 4 * y + (x + d) % 4)

    far = 3 - 3 * c
    next_orb = 2 * ((z + 2 * c + 15) % 16) + c

    def n_copy(k):
        return copy((pert, pot)[k], pv.at[far, (x, 4)[k]], ns.at[k], nr.at[k], next_orb, v)

    def f_copy(d):
        return copy(pv.at[far, x], pv.at[far, x], fs.at[d - 1], fr.at[d - 1], o, 4 * y + (x + d) % 4)

    def h_copy(k):
        slab = (own, far)[k]
        return copy(pv.at[slab], pv.at[slab], hs.at[k], hr.at[k], mate, v)

    n_copy(0).start()
    n_copy(1).start()
    for d in (2, 1, 3):
        x_copy(d).start()

    @pl.when(x != 0)
    def _():
        z_copy(0).start()
        e_copy(0).start()

    @pl.when(x == 0)
    def _():
        psi_all[y, 0] = psi_in[0]
        en_all[0] = energy[...]

    for q in ZORDER[1:]:
        z_copy(q).start()
        e_copy(q).start()

    def y_copy(q, d):
        return copy(psi_all.at[y, q], psi_all.at[y, q], ys.at[3 * q + d - 1], yr.at[3 * q + d - 1], o, 4 * ((y + d) % 4) + x)

    def spread(q):
        def arrived():
            z_copy(q).wait()
            e_copy(q).wait()

        if q == 0:
            pl.when(x != 0)(arrived)
        else:
            arrived()
        for d in (2, 1, 3):
            y_copy(q, d).start()

    lane = lax.broadcasted_iota(jnp.int32, (24, 128), 1)

    def vector(n):
        return (x + jnp.where(n == 0, 2, jnp.where(n == 1, 1, jnp.where(n == 2, 3, 0)))) % 4

    def half_copy(n):
        return copy(pk.at[1 - c, vector(n)], rc.at[vector(n)], cs.at[n], cr.at[n], mate, v)

    def r_copy(n):
        return copy(rd.at[vector(n)], rx.at[n], rs.at[n], rr.at[n], o, 4 * y + vector(n))

    def finish(n):
        half_copy(n).wait()
        rd[vector(n)] = pk[c, vector(n)] + rc[vector(n)]

    def reduce(n):
        k = vector(n)
        for p in range(6):
            f = pack([acc[k, p, s] for s in range(4)], lane)
            for t in range(3):
                pk[p // 3, k, p % 3, :, 128 * t : 128 * t + 128] = f[t]
        half_copy(n).start()

        @pl.when(n > 0)
        def _():
            finish(n - 1)
            r_copy(n - 1).start()

    def prepare(q):
        for d in (1, 2, 3):
            y_copy(q, d).wait()
        level = en_all[q, 0:1, :]

        @pl.loop(0, 12, unroll=4)
        def _(p):
            plane = 6 * z - 3 + p
            half = jnp.where((plane >= 0) & (plane < NZ), 0.5, 0.0)
            psi = unpack(psi_all[p // 3, q, p % 3].astype(F32), lane)
            for s in range(4):
                inverse = 1.0 / (3.25 + potf[p, s] - level)
                cf[p, s] = jnp.where(lane < 96, half * inverse, 0.0)
                pdf[p, s] = -psi[s] * inverse
                psif[p, s] = psi[s]

    def solve(q, low, high, after):
        def stencil(f, p):
            mid = [f[p, s, 8:32, :] for s in range(4)]
            total = []
            for s in range(4):
                up = mid[s - 1] if s > 0 else f[p, 3, 7:31, :]
                down = mid[s + 1] if s < 3 else f[p, 0, 9:33, :]
                n = (f[p - 1, s, 8:32, :] + f[p + 1, s, 8:32, :]) + (up + down)
                n = n + (pltpu.roll(mid[s], 1, 1) + pltpu.roll(mid[s], 127, 1))
                total.append(cf[p, s] * n)
            return mid, total

        @pl.loop(low, high)
        def _(n):
            k = vector(n)

            @pl.loop(0, 12, unroll=12)
            def _(p):
                for s in range(4):
                    gf[p, s, 8:32, :] = vf[k, p, s] * pdf[p, s]

            @pl.loop(1, 11, unroll=10)
            def _(p):
                mid, total = stencil(gf, p)
                for s in range(4):
                    hf[p, s, 8:32, :] = mid[s] + total[s]

            @pl.loop(2, 10, unroll=8)
            def _(p):
                _, total = stencil(hf, p)
                for s in range(4):
                    mf[p, s, 8:32, :] = total[s]

            @pl.loop(3, 9, unroll=6)
            def _(p):
                _, total = stencil(mf, p)
                for s in range(4):
                    answer = (SCALE * Q0) * hf[p, s, 8:32, :] + (SCALE * Q2) * total[s]
                    acc[k, p - 3, s] = acc[k, p - 3, s] + psif[p, s] * answer

            if after is not None:
                after(n)

    def widen(slab):
        @pl.loop(0, 3)
        def _(n):
            p = 3 * slab + n
            for k in range(5):
                field = unpack(pv[slab, k, n].astype(F32), lane)
                for s in range(4):
                    if k < 4:
                        vf[k, p, s] = field[s]
                    else:
                        potf[p, s] = field[s]

    n_copy(0).wait()
    n_copy(1).wait()
    for d in (2, 1, 3):
        f_copy(d).start()
    for d in (1, 2, 3):
        x_copy(d).wait()
    h_copy(0).start()
    spread(0)
    spread(2)
    widen(own)
    for d in (1, 2, 3):
        f_copy(d).wait()
    h_copy(1).start()
    widen(far)
    h_copy(0).wait()
    widen(2 - c)
    h_copy(1).wait()
    widen(3 * c)
    prepare(0)
    solve(0, 0, 2, None)
    spread(1)
    spread(3)
    solve(0, 2, 4, None)
    prepare(2)
    solve(2, 0, 4, None)
    prepare(1)
    solve(1, 0, 4, None)
    prepare(3)
    solve(3, 0, 4, reduce)
    finish(3)
    for n in range(3):
        r_copy(n).wait()

    def halves(a):
        high = a.astype(BF16)
        return high, (a - high.astype(F32)).astype(BF16)

    def dot(a, b, dims=(((1,), (0,)), ((), ()))):
        a_high, a_low = a if isinstance(a, tuple) else halves(a)
        b_high, b_low = halves(b)

        def product(l, r):
            return lax.dot_general(l, r, dims, preferred_element_type=F32)

        return product(a_high, b_high) + (product(a_high, b_low) + product(a_low, b_high))

    load_small.wait()
    load_kz.wait()
    for p in range(3):
        total = (rd[x, p] + rx[0, p]) + (rx[1, p] + rx[2, p])
        plane = jnp.concatenate(unpack(total, lane), axis=0)
        plane = dot(small[2, :, :96], dot(plane, small[p // 2]))
        x1[:, p] = plane.reshape(16, 8, 128)

    def layer_exchange(src, dst, send, recv):
        def one(d):
            to = (v + d) % 16
            return copy(src.at[to], dst.at[v], send, recv, o, to)

        @pl.loop(1, 16)
        def _(d):
            one(d).start()

        dst[v] = src[v]
        copy(src.at[pl.ds(0, 15)], dst.at[pl.ds(0, 15)], send, recv, o, (v + 1) % 16).wait()

    layer_exchange(x1, y1, a1s, a1r)

    def column_start(src, dst, send, recv):
        def one(d):
            to = (o + d) % 32
            return copy(src.at[to], dst.at[o], send, recv, to, v)

        @pl.loop(1, 32)
        def _(d):
            one(d).start()

        dst[o] = src[o]
        return copy(src.at[pl.ds(0, 31)], dst.at[pl.ds(0, 31)], send, recv, (o + 1) % 32, v)

    big = (128, 128)
    slot = lax.broadcasted_iota(jnp.int32, big, 0) % 4
    lanes = lax.broadcasted_iota(jnp.int32, big, 1)
    i = lanes % 8
    across = (((1,), (1,)), ((), ()))
    same = lax.broadcasted_iota(jnp.int32, big, 0) % 8 == i

    def spare(f0, f1, f2):
        moved = jnp.where(slot == 1, pltpu.roll(f1, 4, 1), jnp.where(slot == 2, pltpu.roll(f2, 2, 1), 0.0))
        moved = jnp.where(slot == 0, pltpu.roll(f0, 6, 1), moved)
        return jnp.where(i >= 6, moved, 0.0)

    p0, p1, p2 = [y1[:, p].reshape(big).T for p in range(3)]
    up1, up2 = pltpu.roll(p2, 1, 0), pltpu.roll(p2, 2, 0)
    u1[:, 0] = (p0 + jnp.where(slot == 3, p2, 0.0) + spare(p2, up1, up2)).reshape(32, 4, 128)
    u1[:, 1] = (p1 + jnp.where(slot == 3, up1, 0.0)).reshape(32, 4, 128)
    first = column_start(u1, w1, b1s, b1r)
    first.wait()
    half_a, half_b = w1[:, 0].reshape(big), w1[:, 1].reshape(big)
    back = jnp.where((slot == 1) & (i >= 2) & (i < 4), pltpu.roll(half_a, 124, 1), 0.0)
    back = jnp.where((slot == 2) & (i >= 4) & (i < 6), pltpu.roll(half_a, 126, 1), back)
    back = jnp.where((slot == 0) & (i < 2), pltpu.roll(half_a, 122, 1), back)
    spectral = dot((kz[0], kz[1]), jnp.concatenate([half_a, half_b, back], axis=0)) * damp[...]

    full = dot(spectral, spectral, (((0,), (0,)), ((), ())))
    full = jnp.sum(jnp.where(same, full, 0.0).reshape(16, 8, 128), axis=1)
    gram = dot(full, small[4])
    mine = 2 * v + c
    t1[mine] = gram[:8] + pltpu.roll(gram[8:], 16, 1)

    def g1_copy(d, other):
        to = (v + d) % 16
        orb = mate if other else o
        return copy(t1.at[mine], t1.at[mine], g1s, g1r, orb, to)

    g1_copy(0, 1).start()

    @pl.loop(1, 16)
    def _(d):
        g1_copy(d, 0).start()
        g1_copy(d, 1).start()

    columns = dot((kz[2], kz[3]), spectral)
    extra = columns[256:]
    u2[:, 0] = (columns[:128] + spare(extra, extra, extra)).reshape(32, 4, 128)
    u2[:, 1] = columns[128:256].reshape(32, 4, 128)
    second = column_start(u2, w2, b2s, b2r)
    copy(t1.at[pl.ds(0, 31)], t1.at[pl.ds(0, 31)], g1s, g1r, mate, v).wait()
    t2[z] = jnp.sum(t1[...], axis=0)

    def g2_copy(d):
        return copy(t2.at[z], t2.at[z], g2s, g2r, 2 * ((z + d) % 16) + c, v)

    @pl.loop(1, 16)
    def _(d):
        g2_copy(d).start()

    copy(t2.at[pl.ds(0, 15)], t2.at[pl.ds(0, 15)], g2s, g2r, 2 * ((z + 1) % 16) + c, v).wait()
    folded = jnp.sum(t2[...], axis=0) * (1.0 / (NZ * NYX))
    row = lax.broadcasted_iota(jnp.int32, (16, 128), 0)
    col = lax.broadcasted_iota(jnp.int32, (16, 128), 1)
    work = jnp.concatenate([folded, pltpu.roll(folded, 112, 1)], axis=0)
    work = jnp.where(col < 16, work, jnp.where(col == row + 16, 1.0, 0.0))

    for j in range(15):
        column = jnp.broadcast_to(work[:, j : j + 1], (16, 128))
        ratio = work[j : j + 1, :] * (1.0 / column[j : j + 1, :])
        work = work - jnp.where(row > j, column, 0.0) * ratio
    pivots = jnp.sum(jnp.where(col == row, work, 0.0), axis=1, keepdims=True)
    work = work * (1.0 / jnp.sqrt(pivots))
    factor[...] = jnp.where(col >= row, work, 0.0)[:, :16]
    right = jnp.where(col < 16, pltpu.roll(work, 112, 1), 0.0)
    right = dot(right, small[4], across)
    mix = jnp.broadcast_to(right[:, None, :], (16, 8, 128)).reshape(big)
    mix = jnp.where(same, mix, 0.0)

    second.wait()
    half_a, half_b = w2[:, 0].reshape(big), w2[:, 1].reshape(big)
    back = jnp.where(i < 4, pltpu.roll(pltpu.roll(half_a, 127, 0), 124, 1), pltpu.roll(pltpu.roll(half_a, 126, 0), 126, 1))
    back = jnp.where(i < 2, pltpu.roll(half_a, 122, 1), back)
    third = jnp.where(slot == 3, half_a, jnp.where(slot == 2, pltpu.roll(half_b, 127, 0), 0.0))
    third = jnp.where(slot == 0, jnp.where(i < 6, back, 0.0), third)
    for p, plane in enumerate((half_a, half_b, third)):
        x2[:, p] = dot(mix, plane, across).reshape(16, 8, 128)
    layer_exchange(x2, y2, a2s, a2r)
    for p in range(3):
        flat = y2[:, p].reshape(128, 128)
        plane = dot(dot(small[3, :96, :], flat), small[p // 2], across)
        f = pack([plane[24 * s : 24 * s + 24] for s in range(4)], lane)
        for t in range(3):
            out[p, :, 128 * t : 128 * t + 128] = f[t]


def body(orbitals, energies, trial_potential, local_potential):
    o = lax.axis_index("orb")
    v = lax.axis_index("vec")
    z = o // 2
    y, x = v // 4, v % 4
    wanted = []
    for q in range(4):
        to = (z + 16 - offset(x, q)) % 16
        wanted.append(6 * to - 3 + 3 * y)
    at = jnp.concatenate([w + jnp.arange(3) for w in wanted])
    pickz = (at[:, None] == jnp.arange(NZ)[None, :]).astype(BF16)
    pieces = jnp.dot(pickz, orbitals[0], preferred_element_type=F32).astype(BF16)
    psi_in = pieces.reshape(4, 3, 24, 384)
    pert = trial_potential.reshape(3, 24, 384)
    pot = local_potential.reshape(3, 24, 384)
    small, kz = tables()
    vmem = pl.BlockSpec(memory_space=pltpu.VMEM)
    dma = pltpu.SemaphoreType.DMA
    piece = (3, 24, 384)
    blocks = (12, 4, 24, 128)
    ortho, factor = pl.pallas_call(
        kernel,
        out_shape=(
            jax.ShapeDtypeStruct(piece, F32),
            jax.ShapeDtypeStruct((16, 16), F32),
        ),
        in_specs=[vmem] * 4 + [pl.BlockSpec(memory_space=pltpu.HBM)] * 2,
        out_specs=(vmem, vmem),
        scratch_shapes=[
            pltpu.VMEM((5, 128, 128), F32),
            pltpu.VMEM((4, 384, 384), BF16),
            pltpu.VMEM((384, 128), F32),
            pltpu.VMEM((8, 128), F32),
            pltpu.VMEM((4, 4) + piece, BF16),
            pltpu.VMEM((4, 8, 128), F32),
            pltpu.VMEM((4, 5) + piece, BF16),
            pltpu.VMEM((4,) + blocks, F32),
            pltpu.VMEM(blocks, F32),
            pltpu.VMEM(blocks, F32),
            pltpu.VMEM(blocks, F32),
            pltpu.VMEM(blocks, F32),
            pltpu.VMEM((12, 4, 40, 128), F32),
            pltpu.VMEM((12, 4, 40, 128), F32),
            pltpu.VMEM((12, 4, 40, 128), F32),
            pltpu.VMEM((4, 6, 4, 24, 128), F32),
            pltpu.VMEM((2, 4) + piece, F32),
            pltpu.VMEM((4,) + piece, F32),
            pltpu.VMEM((4,) + piece, F32),
            pltpu.VMEM((3,) + piece, F32),
            pltpu.VMEM((16, 3, 8, 128), F32),
            pltpu.VMEM((16, 3, 8, 128), F32),
            pltpu.VMEM((32, 2, 4, 128), F32),
            pltpu.VMEM((32, 2, 4, 128), F32),
            pltpu.VMEM((32, 2, 4, 128), F32),
            pltpu.VMEM((32, 2, 4, 128), F32),
            pltpu.VMEM((16, 3, 8, 128), F32),
            pltpu.VMEM((16, 3, 8, 128), F32),
            pltpu.VMEM((32, 8, 128), F32),
            pltpu.VMEM((16, 8, 128), F32),
            dma((4,)), dma((4,)), dma((4,)), dma((4,)), dma((3,)), dma((3,)), dma((2,)), dma((2,)), dma((3,)), dma((3,)), dma((2,)), dma((2,)),
            dma((12,)), dma((12,)), dma((4,)), dma((4,)), dma((3,)), dma((3,)),
            *([dma(())] * 12), dma((2,)),
        ],
        compiler_params=pltpu.CompilerParams(
            collective_id=0, has_side_effects=True, vmem_limit_bytes=48 << 20
        ),
    )(psi_in, pert, pot, energies.reshape(1, 1), jnp.asarray(small), jnp.asarray(kz))
    return ortho.reshape(1, 3, NYX), factor


def solution(mesh):
    in_specs = (P("orb", None, None), P("orb"), P("vec", "orb", None), P("orb", None))
    out_specs = (P("vec", "orb", None), P())
    return jax.shard_map(body, mesh=mesh, in_specs=in_specs, out_specs=out_specs, check_vma=False)
```

```python
import jax
import jax.numpy as jnp
import numpy as np
from jax import lax
from jax.experimental import pallas as pl
from jax.experimental.pallas import tpu as pltpu
from jax.sharding import PartitionSpec as P

NZ = 96
NY = 96
NX = 96
NYX = 9216
NORB = 32
NV = 16
F32 = jnp.float32
BF16 = jnp.bfloat16
T4 = 8.0 / 0.8**4 - 8.0 / 0.8**2 + 1.0
Q0 = (T4 - 1.0) / T4
Q2 = (8.0 / 0.8**4) / T4
SCALE = 4.0 / NORB
ZORDER = (0, 2, 1, 3)


def sine(n):
    i = np.arange(n, dtype=np.float64) + 1.0
    return np.sqrt(2.0 / (n + 1)) * np.sin(np.pi * i[:, None] * i[None, :] / (n + 1))


def tables():
    s = sine(96)
    row_y = np.arange(96)
    y_of = 4 * (row_y % 24) + row_y // 24
    sx = np.zeros((2, 128, 128))
    a, b, e = np.zeros((3, 96, 4, 32, 4))
    for g in range(32):
        for r in range(3):
            sx[0, :96, 4 * g + r] = s[:, 3 * g + r]
            sx[1, :96, 4 * g + (3, 2, 0)[r]] = s[:, 3 * g + r]
            a[:, r, g, r] = s[:, 3 * g]
            b[:, r, g, r] = s[:, 3 * g + 1]
            e[:, 2, g, r] = s[:, 3 * g + 2]
        a[:, 0, g, 3] = s[:, 3 * g + 2]
        b[:, 1, g, 3] = s[:, 3 * g + 2]
    sy = np.zeros((128, 128))
    for w in range(16):
        for i in range(6):
            sy[8 * w + i, :96] = s[6 * w + i, y_of]
    pick = np.zeros((128, 128))
    pick[np.arange(128), np.arange(128) // 8] = 1.0
    small = np.stack([sx[0], sx[1], sy, sy.T, pick])
    kz = np.concatenate([m.reshape(384, 128) for m in (a, b, e)], axis=1)
    kz_high = kz.astype(BF16)
    kz_low = (kz - kz_high.astype(np.float64)).astype(BF16)
    return small.astype(np.float32), np.stack([kz_high, kz_low, kz_high.T, kz_low.T])


def offset(x, q):
    base = 8 * (q % 2)
    if q < 2:
        return base + x
    return (base + 16 - x + jnp.where(x == 0, 4, 0)) % 16


def unpack(packed, lane):
    f0, f1, f2 = packed[:, :128], packed[:, 128:256], packed[:, 256:]
    y0 = jnp.where(lane < 96, f0, 0.0)
    y1 = jnp.where(lane < 32, pltpu.roll(f0, 32, 1), jnp.where(lane < 96, pltpu.roll(f1, 32, 1), 0.0))
    y2 = jnp.where(lane < 64, pltpu.roll(f1, 64, 1), jnp.where(lane < 96, pltpu.roll(f2, 64, 1), 0.0))
    y3 = jnp.where(lane < 96, pltpu.roll(f2, 96, 1), 0.0)
    return y0, y1, y2, y3


def pack(y, lane):
    r1, r2, r3 = pltpu.roll(y[1], 96, 1), pltpu.roll(y[2], 64, 1), pltpu.roll(y[3], 32, 1)
    return (
        jnp.where(lane < 96, y[0], r1),
        jnp.where(lane < 64, r1, r2),
        jnp.where(lane < 32, r2, r3),
    )


def kernel(
    psi_in, pert, pot, level_ref, small_hbm, kz_hbm, out, factor,
    small, kz, tri, damp, energy, psi_all, en_all, pv, vf, potf, cf, pdf, psif, gf, hf, mf, acc,
    pk, rc, rd, rx, x1, y1, u1, w1, u2, w2, x2, y2, t1, t2,
    zs, zr, es, er, xs, xr, ns, nr, fs, fr, hs, hr, ys, yr, cs, cr, rs, rr,
    a1s, a1r, b1s, b1r, b2s, b2r, g1s, g1r, g2s, g2r, a2s, a2r, ks,
):
    o = lax.axis_index("orb")
    v = lax.axis_index("vec")
    z, c = o // 2, o % 2
    y, x = v // 4, v % 4
    mate = 2 * z + 1 - c

    def copy(src, dst, send, recv, orb, vec):
        return pltpu.make_async_remote_copy(
            src_ref=src, dst_ref=dst, send_sem=send, recv_sem=recv,
            device_id={"orb": orb, "vec": vec}, device_id_type=pl.DeviceIdType.MESH,
        )

    barrier = pltpu.get_barrier_semaphore()

    def greet(orb, vec):
        pl.semaphore_signal(
            barrier, inc=1, device_id={"orb": orb, "vec": vec}, device_id_type=pl.DeviceIdType.MESH
        )

    @pl.loop(1, 32)
    def _(d):
        greet((o + d) % 32, v)

    @pl.loop(1, 16)
    def _(d):
        greet(o, (v + d) % 16)
        greet(mate, (v + d) % 16)

    load_small = pltpu.make_async_copy(small_hbm, small, ks.at[0])
    load_kz = pltpu.make_async_copy(kz_hbm, kz, ks.at[1])
    load_small.start()
    load_kz.start()
    energy[...] = jnp.broadcast_to(level_ref[...], (8, 128))
    own = 1 + c
    pv[own, x] = pert[...]
    pv[own, 4] = pot[...]
    for f in (gf, hf, mf):
        f[:, :, :8, :] = jnp.zeros((12, 4, 8, 128), F32)
        f[:, :, 32:, :] = jnp.zeros((12, 4, 8, 128), F32)
    acc[...] = jnp.zeros(acc.shape, F32)

    to = lax.broadcasted_iota(jnp.int32, (128, 128), 1)
    gap = jnp.abs(to - lax.broadcasted_iota(jnp.int32, (128, 128), 0))
    beside = jnp.where((gap == 1) & (to < 96), 1.0, 0.0).astype(BF16)
    tri[:128, :] = beside
    tri[128:, :] = beside

    def eigen(position):
        return 2.0 - 2.0 * jnp.cos(jnp.pi * (position.astype(F32) + 1.0) / 97)

    r8 = lax.broadcasted_iota(jnp.int32, (8, 128), 0)
    i8 = lax.broadcasted_iota(jnp.int32, (8, 128), 1) % 8
    plane_part = eigen(6 * v + i8) + eigen(3 * o + r8 % 4)
    kept = (i8 < 6) & (r8 % 4 < 3)
    for n in range(48):
        denom = eigen(2 * n + r8 // 4) + plane_part
        damp[8 * n : 8 * n + 8, :] = jnp.where(kept, jnp.sqrt(4.0 * jnp.pi) / jnp.sqrt(denom), 0.0)
    pl.semaphore_wait(barrier, 61)

    def z_copy(q):
        return copy(psi_in.at[q], psi_all.at[y, q], zs.at[q], zr.at[q], 2 * ((z + 16 - offset(x, q)) % 16) + c, v)

    def e_copy(q):
        return copy(energy, en_all.at[q], es.at[q], er.at[q], 2 * ((z + 16 - offset(x, q)) % 16) + c, v)

    def x_copy(d):
        return copy(pert, pv.at[own, x], xs.at[d - 1], xr.at[d - 1], o, 4 * y + (x + d) % 4)

    far = 3 - 3 * c
    next_orb = 2 * ((z + 2 * c + 15) % 16) + c

    def n_copy(k):
        return copy((pert, pot)[k], pv.at[far, (x, 4)[k]], ns.at[k], nr.at[k], next_orb, v)

    def f_copy(d):
        return copy(pv.at[far, x], pv.at[far, x], fs.at[d - 1], fr.at[d - 1], o, 4 * y + (x + d) % 4)

    def h_copy(k):
        slab = (own, far)[k]
        return copy(pv.at[slab], pv.at[slab], hs.at[k], hr.at[k], mate, v)

    n_copy(0).start()
    n_copy(1).start()
    for d in (2, 1, 3):
        x_copy(d).start()

    @pl.when(x != 0)
    def _():
        z_copy(0).start()
        e_copy(0).start()

    @pl.when(x == 0)
    def _():
        psi_all[y, 0] = psi_in[0]
        en_all[0] = energy[...]

    for q in ZORDER[1:]:
        z_copy(q).start()
        e_copy(q).start()

    def y_copy(q, d):
        return copy(psi_all.at[y, q], psi_all.at[y, q], ys.at[3 * q + d - 1], yr.at[3 * q + d - 1], o, 4 * ((y + d) % 4) + x)

    def spread(q):
        def arrived():
            z_copy(q).wait()
            e_copy(q).wait()

        if q == 0:
            pl.when(x != 0)(arrived)
        else:
            arrived()
        for d in (2, 1, 3):
            y_copy(q, d).start()

    lane = lax.broadcasted_iota(jnp.int32, (24, 128), 1)

    def vector(n):
        return (x + jnp.where(n == 0, 2, jnp.where(n == 1, 1, jnp.where(n == 2, 3, 0)))) % 4

    def half_copy(n):
        return copy(pk.at[1 - c, vector(n)], rc.at[vector(n)], cs.at[n], cr.at[n], mate, v)

    def r_copy(n):
        return copy(rd.at[vector(n)], rx.at[n], rs.at[n], rr.at[n], o, 4 * y + vector(n))

    def finish(n):
        half_copy(n).wait()
        rd[vector(n)] = pk[c, vector(n)] + rc[vector(n)]

    def reduce(n):
        k = vector(n)
        for p in range(6):
            f = pack([acc[k, p, s] for s in range(4)], lane)
            for t in range(3):
                pk[p // 3, k, p % 3, :, 128 * t : 128 * t + 128] = f[t]
        half_copy(n).start()

        @pl.when(n > 0)
        def _():
            finish(n - 1)
            r_copy(n - 1).start()

    def prepare(q):
        for d in (1, 2, 3):
            y_copy(q, d).wait()
        level = en_all[q, 0:1, :]

        @pl.loop(0, 12, unroll=4)
        def _(p):
            plane = 6 * z - 3 + p
            half = jnp.where((plane >= 0) & (plane < NZ), 0.5, 0.0)
            psi = unpack(psi_all[p // 3, q, p % 3].astype(F32), lane)
            for s in range(4):
                inverse = 1.0 / (3.25 + potf[p, s] - level)
                cf[p, s] = jnp.where(lane < 96, half * inverse, 0.0)
                pdf[p, s] = -psi[s] * inverse
                psif[p, s] = psi[s]

    def solve(q, low, high, after):
        def stencil(f, p):
            mid = [f[p, s, 8:32, :] for s in range(4)]
            total = []
            whole = jnp.concatenate(mid[2:], axis=0)
            whole_high = whole.astype(BF16)
            whole_low = (whole - whole_high.astype(F32)).astype(BF16)
            beside = jnp.dot(jnp.concatenate([whole_high, whole_low], axis=1), tri[...], preferred_element_type=F32)
            for s in range(4):
                up = mid[s - 1] if s > 0 else f[p, 3, 7:31, :]
                down = mid[s + 1] if s < 3 else f[p, 0, 9:33, :]
                n = (f[p - 1, s, 8:32, :] + f[p + 1, s, 8:32, :]) + (up + down)
                if s < 2:
                    n = n + (pltpu.roll(mid[s], 1, 1) + pltpu.roll(mid[s], 127, 1))
                else:
                    n = n + beside[24 * s - 48 : 24 * s - 24]
                total.append(cf[p, s] * n)
            return mid, total

        @pl.loop(low, high)
        def _(n):
            k = vector(n)

            @pl.loop(0, 12, unroll=12)
            def _(p):
                for s in range(4):
                    gf[p, s, 8:32, :] = vf[k, p, s] * pdf[p, s]

            @pl.loop(1, 11, unroll=10)
            def _(p):
                mid, total = stencil(gf, p)
                for s in range(4):
                    hf[p, s, 8:32, :] = mid[s] + total[s]

            @pl.loop(2, 10, unroll=8)
            def _(p):
                _, total = stencil(hf, p)
                for s in range(4):
                    mf[p, s, 8:32, :] = total[s]

            @pl.loop(3, 9, unroll=6)
            def _(p):
                _, total = stencil(mf, p)
                for s in range(4):
                    answer = (SCALE * Q0) * hf[p, s, 8:32, :] + (SCALE * Q2) * total[s]
                    acc[k, p - 3, s] = acc[k, p - 3, s] + psif[p, s] * answer

            if after is not None:
                after(n)

    def widen(slab):
        @pl.loop(0, 3)
        def _(n):
            p = 3 * slab + n
            for k in range(5):
                field = unpack(pv[slab, k, n].astype(F32), lane)
                for s in range(4):
                    if k < 4:
                        vf[k, p, s] = field[s]
                    else:
                        potf[p, s] = field[s]

    n_copy(0).wait()
    n_copy(1).wait()
    for d in (2, 1, 3):
        f_copy(d).start()
    for d in (1, 2, 3):
        x_copy(d).wait()
    h_copy(0).start()
    spread(0)
    spread(2)
    widen(own)
    for d in (1, 2, 3):
        f_copy(d).wait()
    h_copy(1).start()
    widen(far)
    h_copy(0).wait()
    widen(2 - c)
    h_copy(1).wait()
    widen(3 * c)
    prepare(0)
    solve(0, 0, 2, None)
    spread(1)
    spread(3)
    solve(0, 2, 4, None)
    prepare(2)
    solve(2, 0, 4, None)
    prepare(1)
    solve(1, 0, 4, None)
    prepare(3)
    solve(3, 0, 4, reduce)
    finish(3)
    for n in range(3):
        r_copy(n).wait()

    def halves(a):
        high = a.astype(BF16)
        return high, (a - high.astype(F32)).astype(BF16)

    def dot(a, b, dims=(((1,), (0,)), ((), ()))):
        a_high, a_low = a if isinstance(a, tuple) else halves(a)
        b_high, b_low = halves(b)

        def product(l, r):
            return lax.dot_general(l, r, dims, preferred_element_type=F32)

        return product(a_high, b_high) + (product(a_high, b_low) + product(a_low, b_high))

    load_small.wait()
    load_kz.wait()
    for p in range(3):
        total = (rd[x, p] + rx[0, p]) + (rx[1, p] + rx[2, p])
        plane = jnp.concatenate(unpack(total, lane), axis=0)
        plane = dot(small[2, :, :96], dot(plane, small[p // 2]))
        x1[:, p] = plane.reshape(16, 8, 128)

    def layer_exchange(src, dst, send, recv):
        def one(d):
            to = (v + d) % 16
            return copy(src.at[to], dst.at[v], send, recv, o, to)

        @pl.loop(1, 16)
        def _(d):
            one(d).start()

        dst[v] = src[v]
        copy(src.at[pl.ds(0, 15)], dst.at[pl.ds(0, 15)], send, recv, o, (v + 1) % 16).wait()

    layer_exchange(x1, y1, a1s, a1r)

    def column_start(src, dst, send, recv):
        def one(d):
            to = (o + d) % 32
            return copy(src.at[to], dst.at[o], send, recv, to, v)

        @pl.loop(1, 32)
        def _(d):
            one(d).start()

        dst[o] = src[o]
        return copy(src.at[pl.ds(0, 31)], dst.at[pl.ds(0, 31)], send, recv, (o + 1) % 32, v)

    big = (128, 128)
    slot = lax.broadcasted_iota(jnp.int32, big, 0) % 4
    lanes = lax.broadcasted_iota(jnp.int32, big, 1)
    i = lanes % 8
    across = (((1,), (1,)), ((), ()))
    same = lax.broadcasted_iota(jnp.int32, big, 0) % 8 == i

    def spare(f0, f1, f2):
        moved = jnp.where(slot == 1, pltpu.roll(f1, 4, 1), jnp.where(slot == 2, pltpu.roll(f2, 2, 1), 0.0))
        moved = jnp.where(slot == 0, pltpu.roll(f0, 6, 1), moved)
        return jnp.where(i >= 6, moved, 0.0)

    p0, p1, p2 = [y1[:, p].reshape(big).T for p in range(3)]
    up1, up2 = pltpu.roll(p2, 1, 0), pltpu.roll(p2, 2, 0)
    u1[:, 0] = (p0 + jnp.where(slot == 3, p2, 0.0) + spare(p2, up1, up2)).reshape(32, 4, 128)
    u1[:, 1] = (p1 + jnp.where(slot == 3, up1, 0.0)).reshape(32, 4, 128)
    first = column_start(u1, w1, b1s, b1r)
    first.wait()
    half_a, half_b = w1[:, 0].reshape(big), w1[:, 1].reshape(big)
    back = jnp.where((slot == 1) & (i >= 2) & (i < 4), pltpu.roll(half_a, 124, 1), 0.0)
    back = jnp.where((slot == 2) & (i >= 4) & (i < 6), pltpu.roll(half_a, 126, 1), back)
    back = jnp.where((slot == 0) & (i < 2), pltpu.roll(half_a, 122, 1), back)
    spectral = dot((kz[0], kz[1]), jnp.concatenate([half_a, half_b, back], axis=0)) * damp[...]

    full = dot(spectral, spectral, (((0,), (0,)), ((), ())))
    full = jnp.sum(jnp.where(same, full, 0.0).reshape(16, 8, 128), axis=1)
    gram = dot(full, small[4])
    mine = 2 * v + c
    t1[mine] = gram[:8] + pltpu.roll(gram[8:], 16, 1)

    def g1_copy(d, other):
        to = (v + d) % 16
        orb = mate if other else o
        return copy(t1.at[mine], t1.at[mine], g1s, g1r, orb, to)

    g1_copy(0, 1).start()

    @pl.loop(1, 16)
    def _(d):
        g1_copy(d, 0).start()
        g1_copy(d, 1).start()

    columns = dot((kz[2], kz[3]), spectral)
    extra = columns[256:]
    u2[:, 0] = (columns[:128] + spare(extra, extra, extra)).reshape(32, 4, 128)
    u2[:, 1] = columns[128:256].reshape(32, 4, 128)
    second = column_start(u2, w2, b2s, b2r)
    copy(t1.at[pl.ds(0, 31)], t1.at[pl.ds(0, 31)], g1s, g1r, mate, v).wait()
    t2[z] = jnp.sum(t1[...], axis=0)

    def g2_copy(d):
        return copy(t2.at[z], t2.at[z], g2s, g2r, 2 * ((z + d) % 16) + c, v)

    @pl.loop(1, 16)
    def _(d):
        g2_copy(d).start()

    copy(t2.at[pl.ds(0, 15)], t2.at[pl.ds(0, 15)], g2s, g2r, 2 * ((z + 1) % 16) + c, v).wait()
    folded = jnp.sum(t2[...], axis=0) * (1.0 / (NZ * NYX))
    row = lax.broadcasted_iota(jnp.int32, (16, 128), 0)
    col = lax.broadcasted_iota(jnp.int32, (16, 128), 1)
    work = jnp.concatenate([folded, pltpu.roll(folded, 112, 1)], axis=0)
    work = jnp.where(col < 16, work, jnp.where(col == row + 16, 1.0, 0.0))

    for j in range(15):
        column = jnp.broadcast_to(work[:, j : j + 1], (16, 128))
        ratio = work[j : j + 1, :] * (1.0 / column[j : j + 1, :])
        work = work - jnp.where(row > j, column, 0.0) * ratio
    pivots = jnp.sum(jnp.where(col == row, work, 0.0), axis=1, keepdims=True)
    work = work * (1.0 / jnp.sqrt(pivots))
    factor[...] = jnp.where(col >= row, work, 0.0)[:, :16]
    right = jnp.where(col < 16, pltpu.roll(work, 112, 1), 0.0)
    right = dot(right, small[4], across)
    mix = jnp.broadcast_to(right[:, None, :], (16, 8, 128)).reshape(big)
    mix = jnp.where(same, mix, 0.0)

    second.wait()
    half_a, half_b = w2[:, 0].reshape(big), w2[:, 1].reshape(big)
    back = jnp.where(i < 4, pltpu.roll(pltpu.roll(half_a, 127, 0), 124, 1), pltpu.roll(pltpu.roll(half_a, 126, 0), 126, 1))
    back = jnp.where(i < 2, pltpu.roll(half_a, 122, 1), back)
    third = jnp.where(slot == 3, half_a, jnp.where(slot == 2, pltpu.roll(half_b, 127, 0), 0.0))
    third = jnp.where(slot == 0, jnp.where(i < 6, back, 0.0), third)
    for p, plane in enumerate((half_a, half_b, third)):
        x2[:, p] = dot(mix, plane, across).reshape(16, 8, 128)
    layer_exchange(x2, y2, a2s, a2r)
    for p in range(3):
        flat = y2[:, p].reshape(128, 128)
        plane = dot(dot(small[3, :96, :], flat), small[p // 2], across)
        f = pack([plane[24 * s : 24 * s + 24] for s in range(4)], lane)
        for t in range(3):
            out[p, :, 128 * t : 128 * t + 128] = f[t]


def body(orbitals, energies, trial_potential, local_potential):
    o = lax.axis_index("orb")
    v = lax.axis_index("vec")
    z = o // 2
    y, x = v // 4, v % 4
    wanted = []
    for q in range(4):
        to = (z + 16 - offset(x, q)) % 16
        wanted.append(6 * to - 3 + 3 * y)
    at = jnp.concatenate([w + jnp.arange(3) for w in wanted])
    pickz = (at[:, None] == jnp.arange(NZ)[None, :]).astype(BF16)
    pieces = jnp.dot(pickz, orbitals[0], preferred_element_type=F32).astype(BF16)
    psi_in = pieces.reshape(4, 3, 24, 384)
    pert = trial_potential.reshape(3, 24, 384)
    pot = local_potential.reshape(3, 24, 384)
    small, kz = tables()
    vmem = pl.BlockSpec(memory_space=pltpu.VMEM)
    dma = pltpu.SemaphoreType.DMA
    piece = (3, 24, 384)
    blocks = (12, 4, 24, 128)
    ortho, factor = pl.pallas_call(
        kernel,
        out_shape=(
            jax.ShapeDtypeStruct(piece, F32),
            jax.ShapeDtypeStruct((16, 16), F32),
        ),
        in_specs=[vmem] * 4 + [pl.BlockSpec(memory_space=pltpu.HBM)] * 2,
        out_specs=(vmem, vmem),
        scratch_shapes=[
            pltpu.VMEM((5, 128, 128), F32),
            pltpu.VMEM((4, 384, 384), BF16),
            pltpu.VMEM((256, 128), BF16),
            pltpu.VMEM((384, 128), F32),
            pltpu.VMEM((8, 128), F32),
            pltpu.VMEM((4, 4) + piece, BF16),
            pltpu.VMEM((4, 8, 128), F32),
            pltpu.VMEM((4, 5) + piece, BF16),
            pltpu.VMEM((4,) + blocks, F32),
            pltpu.VMEM(blocks, F32),
            pltpu.VMEM(blocks, F32),
            pltpu.VMEM(blocks, F32),
            pltpu.VMEM(blocks, F32),
            pltpu.VMEM((12, 4, 40, 128), F32),
            pltpu.VMEM((12, 4, 40, 128), F32),
            pltpu.VMEM((12, 4, 40, 128), F32),
            pltpu.VMEM((4, 6, 4, 24, 128), F32),
            pltpu.VMEM((2, 4) + piece, F32),
            pltpu.VMEM((4,) + piece, F32),
            pltpu.VMEM((4,) + piece, F32),
            pltpu.VMEM((3,) + piece, F32),
            pltpu.VMEM((16, 3, 8, 128), F32),
            pltpu.VMEM((16, 3, 8, 128), F32),
            pltpu.VMEM((32, 2, 4, 128), F32),
            pltpu.VMEM((32, 2, 4, 128), F32),
            pltpu.VMEM((32, 2, 4, 128), F32),
            pltpu.VMEM((32, 2, 4, 128), F32),
            pltpu.VMEM((16, 3, 8, 128), F32),
            pltpu.VMEM((16, 3, 8, 128), F32),
            pltpu.VMEM((32, 8, 128), F32),
            pltpu.VMEM((16, 8, 128), F32),
            dma((4,)), dma((4,)), dma((4,)), dma((4,)), dma((3,)), dma((3,)), dma((2,)), dma((2,)), dma((3,)), dma((3,)), dma((2,)), dma((2,)),
            dma((12,)), dma((12,)), dma((4,)), dma((4,)), dma((3,)), dma((3,)),
            *([dma(())] * 12), dma((2,)),
        ],
        compiler_params=pltpu.CompilerParams(
            collective_id=0, has_side_effects=True, vmem_limit_bytes=48 << 20
        ),
    )(psi_in, pert, pot, energies.reshape(1, 1), jnp.asarray(small), jnp.asarray(kz))
    return ortho.reshape(1, 3, NYX), factor


def solution(mesh):
    in_specs = (P("orb", None, None), P("orb"), P("vec", "orb", None), P("orb", None))
    out_specs = (P("vec", "orb", None), P())
    return jax.shard_map(body, mesh=mesh, in_specs=in_specs, out_specs=out_specs, check_vma=False)
```

```python
import jax
import jax.numpy as jnp
import numpy as np
from jax import lax
from jax.experimental import pallas as pl
from jax.experimental.pallas import tpu as pltpu
from jax.sharding import PartitionSpec as P

NZ = 96
NY = 96
NX = 96
NYX = 9216
NORB = 32
NV = 16
F32 = jnp.float32
BF16 = jnp.bfloat16
T4 = 8.0 / 0.8**4 - 8.0 / 0.8**2 + 1.0
Q0 = (T4 - 1.0) / T4
Q2 = (8.0 / 0.8**4) / T4
SCALE = 4.0 / NORB


def sine(n):
    i = np.arange(n, dtype=np.float64) + 1.0
    return np.sqrt(2.0 / (n + 1)) * np.sin(np.pi * i[:, None] * i[None, :] / (n + 1))


def tables():
    s = sine(96)
    row_y = np.arange(96)
    y_of = 4 * (row_y % 24) + row_y // 24
    sx = np.zeros((2, 128, 128))
    a, b, e = np.zeros((3, 96, 4, 32, 4))
    for g in range(32):
        for r in range(3):
            sx[0, :96, 4 * g + r] = s[:, 3 * g + r]
            sx[1, :96, 4 * g + (3, 2, 0)[r]] = s[:, 3 * g + r]
            a[:, r, g, r] = s[:, 3 * g]
            b[:, r, g, r] = s[:, 3 * g + 1]
            e[:, 2, g, r] = s[:, 3 * g + 2]
        a[:, 0, g, 3] = s[:, 3 * g + 2]
        b[:, 1, g, 3] = s[:, 3 * g + 2]
    sy = np.zeros((128, 128))
    for w in range(16):
        for i in range(6):
            sy[8 * w + i, :96] = s[6 * w + i, y_of]
    pick = np.zeros((128, 128))
    pick[np.arange(128), np.arange(128) // 8] = 1.0
    small = np.stack([sx[0], sx[1], sy, sy.T, pick])
    kz = np.concatenate([m.reshape(384, 128) for m in (a, b, e)], axis=1)
    kz_high = kz.astype(BF16)
    kz_low = (kz - kz_high.astype(np.float64)).astype(BF16)
    return small.astype(np.float32), np.stack([kz_high, kz_low, kz_high.T, kz_low.T])


def offset(x, q):
    base = 8 * (q % 2)
    if q < 2:
        return base + x
    return (base + 16 - x + jnp.where(x == 0, 4, 0)) % 16


def unpack(packed, lane):
    f0, f1, f2 = packed[:, :128], packed[:, 128:256], packed[:, 256:]
    y0 = jnp.where(lane < 96, f0, 0.0)
    y1 = jnp.where(lane < 32, pltpu.roll(f0, 32, 1), jnp.where(lane < 96, pltpu.roll(f1, 32, 1), 0.0))
    y2 = jnp.where(lane < 64, pltpu.roll(f1, 64, 1), jnp.where(lane < 96, pltpu.roll(f2, 64, 1), 0.0))
    y3 = jnp.where(lane < 96, pltpu.roll(f2, 96, 1), 0.0)
    return y0, y1, y2, y3


def pack(y, lane):
    r1, r2, r3 = pltpu.roll(y[1], 96, 1), pltpu.roll(y[2], 64, 1), pltpu.roll(y[3], 32, 1)
    return (
        jnp.where(lane < 96, y[0], r1),
        jnp.where(lane < 64, r1, r2),
        jnp.where(lane < 32, r2, r3),
    )


def kernel(
    psi_in, pert, pot, level_ref, small_hbm, kz_hbm, out, factor,
    small, kz, tri, damp, energy, psi_all, en_all, pv, vf, potf, cf, pdf, psif, gf, hf, mf, acc,
    pk, rc, rd, rx, x1, y1, u1, w1, u2, w2, x2, y2, t1, t2,
    zs, zr, es, er, xs, xr, ns, nr, fs, fr, hs, hr, ys, yr, ps, qs, cs, cr, rs, rr,
    a1s, a1r, b1s, b1r, b2s, b2r, g1s, g1r, g2s, g2r, a2s, a2r, ks,
):
    o = lax.axis_index("orb")
    v = lax.axis_index("vec")
    z, c = o // 2, o % 2
    y, x = v // 4, v % 4
    mate = 2 * z + 1 - c

    def copy(src, dst, send, recv, orb, vec):
        return pltpu.make_async_remote_copy(
            src_ref=src, dst_ref=dst, send_sem=send, recv_sem=recv,
            device_id={"orb": orb, "vec": vec}, device_id_type=pl.DeviceIdType.MESH,
        )

    barrier = pltpu.get_barrier_semaphore()

    def greet(orb, vec):
        pl.semaphore_signal(
            barrier, inc=1, device_id={"orb": orb, "vec": vec}, device_id_type=pl.DeviceIdType.MESH
        )

    @pl.loop(1, 32)
    def _(d):
        greet((o + d) % 32, v)

    @pl.loop(1, 16)
    def _(d):
        greet(o, (v + d) % 16)
        greet(mate, (v + d) % 16)

    load_small = pltpu.make_async_copy(small_hbm, small, ks.at[0])
    load_kz = pltpu.make_async_copy(kz_hbm, kz, ks.at[1])
    load_small.start()
    load_kz.start()
    energy[...] = jnp.broadcast_to(level_ref[...], (8, 128))
    own = 1 + c
    pv[own, x] = pert[...]
    pv[own, 4] = pot[...]
    for f in (gf, hf, mf):
        f[:, :, :8, :] = jnp.zeros((12, 4, 8, 128), F32)
        f[:, :, 32:, :] = jnp.zeros((12, 4, 8, 128), F32)
    acc[...] = jnp.zeros(acc.shape, F32)

    to = lax.broadcasted_iota(jnp.int32, (128, 128), 1)
    gap = jnp.abs(to - lax.broadcasted_iota(jnp.int32, (128, 128), 0))
    beside = jnp.where((gap == 1) & (to < 96), 1.0, 0.0).astype(BF16)
    tri[:128, :] = beside
    tri[128:, :] = beside

    def eigen(position):
        return 2.0 - 2.0 * jnp.cos(jnp.pi * (position.astype(F32) + 1.0) / 97)

    r8 = lax.broadcasted_iota(jnp.int32, (8, 128), 0)
    i8 = lax.broadcasted_iota(jnp.int32, (8, 128), 1) % 8
    plane_part = eigen(6 * v + i8) + eigen(3 * o + r8 % 4)
    kept = (i8 < 6) & (r8 % 4 < 3)
    for n in range(48):
        denom = eigen(2 * n + r8 // 4) + plane_part
        damp[8 * n : 8 * n + 8, :] = jnp.where(kept, jnp.sqrt(4.0 * jnp.pi) / jnp.sqrt(denom), 0.0)
    pl.semaphore_wait(barrier, 61)

    def z_copy(q):
        return copy(psi_in.at[q], psi_all.at[y, q], zs.at[q], zr.at[q], 2 * ((z + 16 - offset(x, q)) % 16) + c, v)

    def plane_copy(q, n):
        at = 6 * (q // 2) + 2 * n
        return copy(
            psi_in.at[q, n], psi_all.at[y, q, n], ps.at[at], ps.at[at + 1],
            2 * ((z + 16 - offset(x, q)) % 16) + c, v,
        )

    def e_copy(q):
        return copy(energy, en_all.at[q], es.at[q], er.at[q], 2 * ((z + 16 - offset(x, q)) % 16) + c, v)

    def x_copy(d):
        return copy(pert, pv.at[own, x], xs.at[d - 1], xr.at[d - 1], o, 4 * y + (x + d) % 4)

    far = 3 - 3 * c
    next_orb = 2 * ((z + 2 * c + 15) % 16) + c

    def n_copy(k):
        return copy((pert, pot)[k], pv.at[far, (x, 4)[k]], ns.at[k], nr.at[k], next_orb, v)

    def f_copy(d):
        return copy(pv.at[far, x], pv.at[far, x], fs.at[d - 1], fr.at[d - 1], o, 4 * y + (x + d) % 4)

    def h_copy(k):
        slab = (own, far)[k]
        return copy(pv.at[slab], pv.at[slab], hs.at[k], hr.at[k], mate, v)

    n_copy(0).start()
    n_copy(1).start()
    for d in (2, 1, 3):
        x_copy(d).start()

    @pl.when(x != 0)
    def _():
        z_copy(0).start()
        e_copy(0).start()

    @pl.when(x == 0)
    def _():
        psi_all[y, 0] = psi_in[0]
        en_all[0] = energy[...]

    z_copy(2).start()
    e_copy(2).start()
    for n in range(3):
        for q in (1, 3):
            plane_copy(q, n).start()
    for q in (1, 3):
        e_copy(q).start()

    def y_copy(q, d):
        return copy(psi_all.at[y, q], psi_all.at[y, q], ys.at[3 * q + d - 1], yr.at[3 * q + d - 1], o, 4 * ((y + d) % 4) + x)

    def part_copy(q, n, d):
        at = 2 * (9 * (q // 2) + 3 * n + d - 1)
        return copy(
            psi_all.at[y, q, n], psi_all.at[y, q, n], qs.at[at], qs.at[at + 1], o, 4 * ((y + d) % 4) + x
        )

    def spread_plane(n):
        for q in (1, 3):
            plane_copy(q, n).wait()
            for d in (2, 1, 3):
                part_copy(q, n, d).start()

    def spread(q):
        def arrived():
            z_copy(q).wait()
            e_copy(q).wait()

        if q == 0:
            pl.when(x != 0)(arrived)
        else:
            arrived()
        for d in (2, 1, 3):
            y_copy(q, d).start()

    lane = lax.broadcasted_iota(jnp.int32, (24, 128), 1)

    def vector(n):
        return (x + jnp.where(n == 0, 2, jnp.where(n == 1, 1, jnp.where(n == 2, 3, 0)))) % 4

    def half_copy(n):
        return copy(pk.at[1 - c, vector(n)], rc.at[vector(n)], cs.at[n], cr.at[n], mate, v)

    def r_copy(n):
        return copy(rd.at[vector(n)], rx.at[n], rs.at[n], rr.at[n], o, 4 * y + vector(n))

    def finish(n):
        half_copy(n).wait()
        rd[vector(n)] = pk[c, vector(n)] + rc[vector(n)]

    def reduce(n):
        k = vector(n)
        for p in range(6):
            f = pack([acc[k, p, s] for s in range(4)], lane)
            for t in range(3):
                pk[p // 3, k, p % 3, :, 128 * t : 128 * t + 128] = f[t]
        half_copy(n).start()

        @pl.when(n > 0)
        def _():
            finish(n - 1)
            r_copy(n - 1).start()

    def prepare(q):
        for d in (1, 2, 3):
            if q % 2 == 0:
                y_copy(q, d).wait()
            else:
                for n in range(3):
                    part_copy(q, n, d).wait()
        if q % 2 == 1:
            e_copy(q).wait()
        level = en_all[q, 0:1, :]

        @pl.loop(0, 12, unroll=4)
        def _(p):
            plane = 6 * z - 3 + p
            half = jnp.where((plane >= 0) & (plane < NZ), 0.5, 0.0)
            psi = unpack(psi_all[p // 3, q, p % 3].astype(F32), lane)
            for s in range(4):
                inverse = 1.0 / (3.25 + potf[p, s] - level)
                cf[p, s] = jnp.where(lane < 96, half * inverse, 0.0)
                pdf[p, s] = -psi[s] * inverse
                psif[p, s] = psi[s]

    def solve(q, low, high, after):
        def stencil(f, p):
            mid = [f[p, s, 8:32, :] for s in range(4)]
            total = []
            whole = jnp.concatenate(mid[2:], axis=0)
            whole_high = whole.astype(BF16)
            whole_low = (whole - whole_high.astype(F32)).astype(BF16)
            beside = jnp.dot(jnp.concatenate([whole_high, whole_low], axis=1), tri[...], preferred_element_type=F32)
            for s in range(4):
                up = mid[s - 1] if s > 0 else f[p, 3, 7:31, :]
                down = mid[s + 1] if s < 3 else f[p, 0, 9:33, :]
                n = (f[p - 1, s, 8:32, :] + f[p + 1, s, 8:32, :]) + (up + down)
                if s < 2:
                    n = n + (pltpu.roll(mid[s], 1, 1) + pltpu.roll(mid[s], 127, 1))
                else:
                    n = n + beside[24 * s - 48 : 24 * s - 24]
                total.append(cf[p, s] * n)
            return mid, total

        @pl.loop(low, high)
        def _(n):
            k = vector(n)

            @pl.loop(0, 12, unroll=12)
            def _(p):
                for s in range(4):
                    gf[p, s, 8:32, :] = vf[k, p, s] * pdf[p, s]

            @pl.loop(1, 11, unroll=10)
            def _(p):
                mid, total = stencil(gf, p)
                for s in range(4):
                    hf[p, s, 8:32, :] = mid[s] + total[s]

            @pl.loop(2, 10, unroll=8)
            def _(p):
                _, total = stencil(hf, p)
                for s in range(4):
                    mf[p, s, 8:32, :] = total[s]

            @pl.loop(3, 9, unroll=6)
            def _(p):
                _, total = stencil(mf, p)
                for s in range(4):
                    answer = (SCALE * Q0) * hf[p, s, 8:32, :] + (SCALE * Q2) * total[s]
                    acc[k, p - 3, s] = acc[k, p - 3, s] + psif[p, s] * answer

            if after is not None:
                after(n)

    def widen(slab):
        @pl.loop(0, 3)
        def _(n):
            p = 3 * slab + n
            for k in range(5):
                field = unpack(pv[slab, k, n].astype(F32), lane)
                for s in range(4):
                    if k < 4:
                        vf[k, p, s] = field[s]
                    else:
                        potf[p, s] = field[s]

    n_copy(0).wait()
    n_copy(1).wait()
    for d in (2, 1, 3):
        f_copy(d).start()
    for d in (1, 2, 3):
        x_copy(d).wait()
    h_copy(0).start()
    spread(0)
    spread(2)
    widen(own)
    for d in (1, 2, 3):
        f_copy(d).wait()
    h_copy(1).start()
    widen(far)
    h_copy(0).wait()
    widen(2 - c)
    h_copy(1).wait()
    spread_plane(0)
    widen(3 * c)
    prepare(0)
    spread_plane(1)
    solve(0, 0, 2, None)
    spread_plane(2)
    solve(0, 2, 4, None)
    prepare(2)
    solve(2, 0, 4, None)
    prepare(1)
    solve(1, 0, 4, None)
    prepare(3)
    solve(3, 0, 4, reduce)
    finish(3)
    for n in range(3):
        r_copy(n).wait()

    def halves(a):
        high = a.astype(BF16)
        return high, (a - high.astype(F32)).astype(BF16)

    def dot(a, b, dims=(((1,), (0,)), ((), ()))):
        a_high, a_low = a if isinstance(a, tuple) else halves(a)
        b_high, b_low = halves(b)

        def product(l, r):
            return lax.dot_general(l, r, dims, preferred_element_type=F32)

        return product(a_high, b_high) + (product(a_high, b_low) + product(a_low, b_high))

    load_small.wait()
    load_kz.wait()
    for p in range(3):
        total = (rd[x, p] + rx[0, p]) + (rx[1, p] + rx[2, p])
        plane = jnp.concatenate(unpack(total, lane), axis=0)
        plane = dot(small[2, :, :96], dot(plane, small[p // 2]))
        x1[:, p] = plane.reshape(16, 8, 128)

    def layer_exchange(src, dst, send, recv):
        def one(d):
            to = (v + d) % 16
            return copy(src.at[to], dst.at[v], send, recv, o, to)

        @pl.loop(1, 16)
        def _(d):
            one(d).start()

        dst[v] = src[v]
        copy(src.at[pl.ds(0, 15)], dst.at[pl.ds(0, 15)], send, recv, o, (v + 1) % 16).wait()

    layer_exchange(x1, y1, a1s, a1r)

    def column_start(src, dst, send, recv):
        def one(d):
            to = (o + d) % 32
            return copy(src.at[to], dst.at[o], send, recv, to, v)

        @pl.loop(1, 32)
        def _(d):
            one(d).start()

        dst[o] = src[o]
        return copy(src.at[pl.ds(0, 31)], dst.at[pl.ds(0, 31)], send, recv, (o + 1) % 32, v)

    big = (128, 128)
    slot = lax.broadcasted_iota(jnp.int32, big, 0) % 4
    lanes = lax.broadcasted_iota(jnp.int32, big, 1)
    i = lanes % 8
    across = (((1,), (1,)), ((), ()))
    same = lax.broadcasted_iota(jnp.int32, big, 0) % 8 == i

    def spare(f0, f1, f2):
        moved = jnp.where(slot == 1, pltpu.roll(f1, 4, 1), jnp.where(slot == 2, pltpu.roll(f2, 2, 1), 0.0))
        moved = jnp.where(slot == 0, pltpu.roll(f0, 6, 1), moved)
        return jnp.where(i >= 6, moved, 0.0)

    p0, p1, p2 = [y1[:, p].reshape(big).T for p in range(3)]
    up1, up2 = pltpu.roll(p2, 1, 0), pltpu.roll(p2, 2, 0)
    u1[:, 0] = (p0 + jnp.where(slot == 3, p2, 0.0) + spare(p2, up1, up2)).reshape(32, 4, 128)
    u1[:, 1] = (p1 + jnp.where(slot == 3, up1, 0.0)).reshape(32, 4, 128)
    first = column_start(u1, w1, b1s, b1r)
    first.wait()
    half_a, half_b = w1[:, 0].reshape(big), w1[:, 1].reshape(big)
    back = jnp.where((slot == 1) & (i >= 2) & (i < 4), pltpu.roll(half_a, 124, 1), 0.0)
    back = jnp.where((slot == 2) & (i >= 4) & (i < 6), pltpu.roll(half_a, 126, 1), back)
    back = jnp.where((slot == 0) & (i < 2), pltpu.roll(half_a, 122, 1), back)
    spectral = dot((kz[0], kz[1]), jnp.concatenate([half_a, half_b, back], axis=0)) * damp[...]

    full = dot(spectral, spectral, (((0,), (0,)), ((), ())))
    full = jnp.sum(jnp.where(same, full, 0.0).reshape(16, 8, 128), axis=1)
    gram = dot(full, small[4])
    mine = 2 * v + c
    t1[mine] = gram[:8] + pltpu.roll(gram[8:], 16, 1)

    def g1_copy(d, other):
        to = (v + d) % 16
        orb = mate if other else o
        return copy(t1.at[mine], t1.at[mine], g1s, g1r, orb, to)

    g1_copy(0, 1).start()

    @pl.loop(1, 16)
    def _(d):
        g1_copy(d, 0).start()
        g1_copy(d, 1).start()

    columns = dot((kz[2], kz[3]), spectral)
    extra = columns[256:]
    u2[:, 0] = (columns[:128] + spare(extra, extra, extra)).reshape(32, 4, 128)
    u2[:, 1] = columns[128:256].reshape(32, 4, 128)
    second = column_start(u2, w2, b2s, b2r)
    copy(t1.at[pl.ds(0, 31)], t1.at[pl.ds(0, 31)], g1s, g1r, mate, v).wait()
    t2[z] = jnp.sum(t1[...], axis=0)

    def g2_copy(d):
        return copy(t2.at[z], t2.at[z], g2s, g2r, 2 * ((z + d) % 16) + c, v)

    @pl.loop(1, 16)
    def _(d):
        g2_copy(d).start()

    copy(t2.at[pl.ds(0, 15)], t2.at[pl.ds(0, 15)], g2s, g2r, 2 * ((z + 1) % 16) + c, v).wait()
    folded = jnp.sum(t2[...], axis=0) * (1.0 / (NZ * NYX))
    row = lax.broadcasted_iota(jnp.int32, (16, 128), 0)
    col = lax.broadcasted_iota(jnp.int32, (16, 128), 1)
    work = jnp.concatenate([folded, pltpu.roll(folded, 112, 1)], axis=0)
    work = jnp.where(col < 16, work, jnp.where(col == row + 16, 1.0, 0.0))

    for j in range(15):
        column = jnp.broadcast_to(work[:, j : j + 1], (16, 128))
        ratio = work[j : j + 1, :] * (1.0 / column[j : j + 1, :])
        work = work - jnp.where(row > j, column, 0.0) * ratio
    pivots = jnp.sum(jnp.where(col == row, work, 0.0), axis=1, keepdims=True)
    work = work * (1.0 / jnp.sqrt(pivots))
    factor[...] = jnp.where(col >= row, work, 0.0)[:, :16]
    right = jnp.where(col < 16, pltpu.roll(work, 112, 1), 0.0)
    right = dot(right, small[4], across)
    mix = jnp.broadcast_to(right[:, None, :], (16, 8, 128)).reshape(big)
    mix = jnp.where(same, mix, 0.0)

    second.wait()
    half_a, half_b = w2[:, 0].reshape(big), w2[:, 1].reshape(big)
    back = jnp.where(i < 4, pltpu.roll(pltpu.roll(half_a, 127, 0), 124, 1), pltpu.roll(pltpu.roll(half_a, 126, 0), 126, 1))
    back = jnp.where(i < 2, pltpu.roll(half_a, 122, 1), back)
    third = jnp.where(slot == 3, half_a, jnp.where(slot == 2, pltpu.roll(half_b, 127, 0), 0.0))
    third = jnp.where(slot == 0, jnp.where(i < 6, back, 0.0), third)
    for p, plane in enumerate((half_a, half_b, third)):
        x2[:, p] = dot(mix, plane, across).reshape(16, 8, 128)
    layer_exchange(x2, y2, a2s, a2r)
    for p in range(3):
        flat = y2[:, p].reshape(128, 128)
        plane = dot(dot(small[3, :96, :], flat), small[p // 2], across)
        f = pack([plane[24 * s : 24 * s + 24] for s in range(4)], lane)
        for t in range(3):
            out[p, :, 128 * t : 128 * t + 128] = f[t]


def body(orbitals, energies, trial_potential, local_potential):
    o = lax.axis_index("orb")
    v = lax.axis_index("vec")
    z = o // 2
    y, x = v // 4, v % 4
    wanted = []
    for q in range(4):
        to = (z + 16 - offset(x, q)) % 16
        wanted.append(6 * to - 3 + 3 * y)
    at = jnp.concatenate([w + jnp.arange(3) for w in wanted])
    pickz = (at[:, None] == jnp.arange(NZ)[None, :]).astype(BF16)
    pieces = jnp.dot(pickz, orbitals[0], preferred_element_type=F32).astype(BF16)
    psi_in = pieces.reshape(4, 3, 24, 384)
    pert = trial_potential.reshape(3, 24, 384)
    pot = local_potential.reshape(3, 24, 384)
    small, kz = tables()
    vmem = pl.BlockSpec(memory_space=pltpu.VMEM)
    dma = pltpu.SemaphoreType.DMA
    piece = (3, 24, 384)
    blocks = (12, 4, 24, 128)
    ortho, factor = pl.pallas_call(
        kernel,
        out_shape=(
            jax.ShapeDtypeStruct(piece, F32),
            jax.ShapeDtypeStruct((16, 16), F32),
        ),
        in_specs=[vmem] * 4 + [pl.BlockSpec(memory_space=pltpu.HBM)] * 2,
        out_specs=(vmem, vmem),
        scratch_shapes=[
            pltpu.VMEM((5, 128, 128), F32),
            pltpu.VMEM((4, 384, 384), BF16),
            pltpu.VMEM((256, 128), BF16),
            pltpu.VMEM((384, 128), F32),
            pltpu.VMEM((8, 128), F32),
            pltpu.VMEM((4, 4) + piece, BF16),
            pltpu.VMEM((4, 8, 128), F32),
            pltpu.VMEM((4, 5) + piece, BF16),
            pltpu.VMEM((4,) + blocks, F32),
            pltpu.VMEM(blocks, F32),
            pltpu.VMEM(blocks, F32),
            pltpu.VMEM(blocks, F32),
            pltpu.VMEM(blocks, F32),
            pltpu.VMEM((12, 4, 40, 128), F32),
            pltpu.VMEM((12, 4, 40, 128), F32),
            pltpu.VMEM((12, 4, 40, 128), F32),
            pltpu.VMEM((4, 6, 4, 24, 128), F32),
            pltpu.VMEM((2, 4) + piece, F32),
            pltpu.VMEM((4,) + piece, F32),
            pltpu.VMEM((4,) + piece, F32),
            pltpu.VMEM((3,) + piece, F32),
            pltpu.VMEM((16, 3, 8, 128), F32),
            pltpu.VMEM((16, 3, 8, 128), F32),
            pltpu.VMEM((32, 2, 4, 128), F32),
            pltpu.VMEM((32, 2, 4, 128), F32),
            pltpu.VMEM((32, 2, 4, 128), F32),
            pltpu.VMEM((32, 2, 4, 128), F32),
            pltpu.VMEM((16, 3, 8, 128), F32),
            pltpu.VMEM((16, 3, 8, 128), F32),
            pltpu.VMEM((32, 8, 128), F32),
            pltpu.VMEM((16, 8, 128), F32),
            dma((4,)), dma((4,)), dma((4,)), dma((4,)), dma((3,)), dma((3,)), dma((2,)), dma((2,)), dma((3,)), dma((3,)), dma((2,)), dma((2,)),
            dma((12,)), dma((12,)), dma((12,)), dma((36,)), dma((4,)), dma((4,)), dma((3,)), dma((3,)),
            *([dma(())] * 12), dma((2,)),
        ],
        compiler_params=pltpu.CompilerParams(
            collective_id=0, has_side_effects=True, vmem_limit_bytes=48 << 20
        ),
    )(psi_in, pert, pot, energies.reshape(1, 1), jnp.asarray(small), jnp.asarray(kz))
    return ortho.reshape(1, 3, NYX), factor


def solution(mesh):
    in_specs = (P("orb", None, None), P("orb"), P("vec", "orb", None), P("orb", None))
    out_specs = (P("vec", "orb", None), P())
    return jax.shard_map(body, mesh=mesh, in_specs=in_specs, out_specs=out_specs, check_vma=False)
```
